128 devices in a mesh: row: 8 (over z, x_hi), col: 16 (over x_lo, y, core).
Axes of the slice: x: 4 (x_hi: 2, x_lo: 2; x = x_hi * 2 + x_lo), y: 4, z: 4, core: 2. Of those that a mesh axis runs over, the one named last changes fastest.
Arguments:
- inverse_anc: float32 [8192, 8192], P('row', 'col'), may hold values from -25 to 25, as said below
- factor: float32 [8192, 4096], P('col', 'row'), may hold values from -0.0625 to 0.0625
- pattern: int32 [16, 8], replicated, may hold values 0 or 1
- d_inverse: float32 [4096, 512], P('row'), may hold values from -2 to 2, as said below
- jac_blocks: int32 [32768, 2], P(('row', 'col')), may hold values from 0 to 7, all different within a row; in each aligned block of 256 rows (0 to 255, 256 to 511, ...) at most 128 rows name the same one
- jac_values: float32 [32768, 2, 512], P(('row', 'col')), may hold values from -0.264 to 0.264
Outputs:
- diag_inverse: float32 [4096, 512], P('row')
- variance: float32 [32768], P(('row', 'col'))
The draws below stay inside these ranges and needn't reach their ends.
Inputs may be any that keep to these rules, and one draw needn't show every extreme that they name: `inverse_anc`: exactly symmetric. `d_inverse`: each block exactly symmetric. `jac_blocks`: each row names 2 different panels; among the rows of one device no panel is named more than 128 times, a bound that some block reaches.
All inputs are finite; a program needn't handle non-finite values.
Results may differ from the reference program's by a relative error of at most 0.0003.
Values sent between devices are 32-bit elements; how exact they have to be, the bound alone decides.
No kernel may reach another device: no remote copies, remote signals or barrier semaphores. Data moves between devices by JAX's collectives and lax.ppermute only.
A program may use at most 128 MiB of HBM per device.

```python
import math
import jax
import jax.numpy as jnp
import numpy as np
from jax import lax

P_SIZE = 512
NA = 16
ND = 8
KB = 2
ROWS_DEV = 256
CAP = 128
ROWS = 32768


def draw_inverse_anc(key, part):
    extent = NA * P_SIZE
    key_noise = jax.random.fold_in(key, 11)
    key_diag = jax.random.fold_in(key, 12)
    raw_noise = jax.random.normal(key_noise, (extent, extent), jnp.float32)
    symmetric = (raw_noise + raw_noise.T) * (0.35 / math.sqrt(extent))
    diagonal = jax.random.uniform(key_diag, (extent,), jnp.float32, 1.0, 2.0)
    within = jnp.arange(extent)
    matrix = jnp.where(within[:, None] == within[None, :], diagonal[:, None], symmetric)
    return matrix


def draw_d_inverse(key, part):
    key_noise = jax.random.fold_in(key, 21)
    key_diag = jax.random.fold_in(key, 22)
    raw_noise = jax.random.normal(key_noise, (ND, P_SIZE, P_SIZE), jnp.float32)
    symmetric = (raw_noise + jnp.swapaxes(raw_noise, 1, 2)) * (0.35 / math.sqrt(P_SIZE))
    diagonal = jax.random.uniform(key_diag, (ND, P_SIZE), jnp.float32, 0.5, 1.5)
    within = jnp.arange(P_SIZE)
    matrix = jnp.where((within[:, None] == within[None, :])[None, :, :], diagonal[:, :, None], symmetric)
    return matrix.reshape(ND * P_SIZE, P_SIZE)


def touch_ends(array, stream_key, low, high):
    longest = array.shape.index(max(array.shape))
    spots = []
    for shift in (0, 1):
        where = [jax.random.randint(jax.random.fold_in(stream_key, axis), (), 0, length) for axis, length in enumerate(array.shape)]
        where[longest] = (where[longest] + shift) % array.shape[longest]
        spots.append(tuple(where))
    return array.at[spots[0]].set(low).at[spots[1]].set(high)


def levels(stream_key, dims, cuts, low, high):
    factor_of = 1.0
    for dim, parts in cuts:
        heights = jax.random.uniform(jax.random.fold_in(jax.random.fold_in(stream_key, 6), dim), (parts,), jnp.float32, low / len(cuts), high / len(cuts))
        factor_of = factor_of * jnp.repeat(jnp.exp(heights), dims[dim] // parts).reshape((-1,) + (1,) * (len(dims) - 1 - dim))
    return factor_of


def shared_out(own_key, own, number, rows, amount, top, bound, slope):
    ranking = jax.random.permutation(own_key, amount)
    crowded, usual = load_shares(amount, rows * top, bound, slope, True), load_shares(amount, rows * top, bound, slope, False)
    places = jnp.arange(amount)

    def named(tallies, turn):
        used = int((tallies > 0).sum())
        fixed = max(1, used // 4)
        passed = fixed + (places - fixed + turn * (used - fixed)) % max(1, amount - fixed)
        return jnp.zeros((amount,), jnp.int32).at[ranking[jnp.where(places < fixed, places, passed)]].set(jnp.asarray(tallies, jnp.int32))

    tallies = jnp.where(number % 4 == 0, named(crowded, number // 4), named(usual, number - number // 4 - 1))
    mixed = jax.random.permutation(jax.random.fold_in(own, 3), amount)
    source_of, receiver = mixed[0:amount // 2 * 2:2], mixed[1:amount // 2 * 2:2]
    slack = jnp.minimum(tallies[source_of] - 1, bound - tallies[receiver]) // 2
    slack = jnp.where((source_of == ranking[0]) | (receiver == ranking[0]) | (tallies[receiver] == 0), 0, jnp.maximum(slack, 0))
    passed = jax.random.randint(jax.random.fold_in(own, 4), (amount // 2,), 0, 1 << 20) % (slack + 1)
    tallies = tallies.at[source_of].add(-passed).at[receiver].add(passed)
    items = jnp.searchsorted(jnp.cumsum(tallies), jnp.arange(rows * top), side="right").astype(jnp.int32)
    listing = items.reshape(top, rows).T
    listing = listing[jax.random.permutation(jax.random.fold_in(own, 1), rows)]
    turn = jax.random.randint(jax.random.fold_in(own, 2), (rows, 1), 0, top)
    return jnp.take_along_axis(listing, (jnp.arange(top)[None, :] + turn) % top, axis=1)


def load_shares(amount, total, bound, slope, full):
    weights = [(1 << 20) // math.isqrt(standing ** slope) + 1 for standing in range(1, amount + 1)]
    largest = bound if full else min(bound, max(-(-total // amount), total * weights[0] // sum(weights)))
    least = 1 if total - largest >= amount - 1 else 0
    counts, rest = [largest] + [least] * (amount - 1), total - largest - least * (amount - 1)
    while rest > 0:
        free = [i for i in range(1, amount) if counts[i] < largest] or [i for i in range(1, amount) if counts[i] < bound]
        pool, left = sum([weights[i] for i in free]), rest
        for i in free:
            extra = min(bound - counts[i], max(1, left * weights[i] // pool), rest)
            counts[i] = counts[i] + extra
            rest = rest - extra
    return np.array(counts)


def scatter_about(key, shape, scale, reach, split=(), kind=jnp.bfloat16):
    values = scale * jax.random.normal(key, shape, jnp.float32)
    if split:
        values = values * levels(key, shape, split, -0.22, 0.18)
    return jnp.clip(values, -reach, reach).astype(kind)


def setup_inputs(seed: int = 0) -> dict:
    keys = jax.random.split(jax.random.key(seed), 7)
    inverse_anc = draw_inverse_anc(jax.random.fold_in(keys[6], 71), 0)
    factor = scatter_about(keys[1], (NA * P_SIZE, ND * P_SIZE), (NA * P_SIZE) ** -0.5, 0.0625, ((0, 16), (1, 8)), jnp.float32)
    pattern = touch_ends((jax.random.randint(keys[2], (NA, ND), 0, 2) < 1).astype(jnp.int32), jax.random.fold_in(keys[2], 1), 0, 1)
    d_inverse = draw_d_inverse(jax.random.fold_in(keys[6], 71), 0)
    jac_blocks_keys = jax.random.split(jax.random.fold_in(keys[4], 1), ROWS // ROWS_DEV)
    jac_blocks_turns = jax.random.permutation(jax.random.fold_in(keys[4], 3), ROWS // ROWS_DEV)
    jac_blocks = jax.vmap(lambda own, number: shared_out(jax.random.fold_in(keys[4], 2), own, number, ROWS_DEV, ND, KB, CAP, 2))(jac_blocks_keys, jac_blocks_turns).reshape((ROWS, KB))
    jac_values = scatter_about(keys[5], (ROWS, KB, P_SIZE), 0.044, 0.264, ((0, 128),), jnp.float32)
    return {"inverse_anc": inverse_anc, "factor": factor, "pattern": pattern, "d_inverse": d_inverse, "jac_blocks": jac_blocks, "jac_values": jac_values}


def reference(inverse_anc, factor, pattern, d_inverse, jac_blocks, jac_values):
    block_mask = jnp.repeat(jnp.repeat(pattern.astype(jnp.float32), P_SIZE, axis=0), P_SIZE, axis=1)
    leff = factor * block_mask
    coupled = jnp.dot(inverse_anc, leff, precision=lax.Precision.HIGHEST, preferred_element_type=jnp.float32)

    def increment(block_id):
        left = lax.dynamic_slice_in_dim(leff, block_id * P_SIZE, P_SIZE, 1)
        right = lax.dynamic_slice_in_dim(coupled, block_id * P_SIZE, P_SIZE, 1)
        return jnp.dot(left.T, right, precision=lax.Precision.HIGHEST, preferred_element_type=jnp.float32)

    increments = lax.map(increment, jnp.arange(ND, dtype=jnp.int32))
    diag_inverse = d_inverse + increments.reshape(ND * P_SIZE, P_SIZE)
    blocks = diag_inverse.reshape(ND, P_SIZE, P_SIZE)

    def accumulate(summed, block_id):
        chosen = blocks[block_id]
        projected = jnp.einsum("mkp,pq->mkq", jac_values, chosen, precision=lax.Precision.HIGHEST)
        forms = jnp.sum(projected * jac_values, axis=2)
        return summed + jnp.where(jac_blocks == block_id, forms, jnp.zeros_like(forms)), None

    summed, _ = lax.scan(accumulate, jnp.zeros(jac_blocks.shape, jnp.float32), jnp.arange(ND, dtype=jnp.int32))
    variance = jnp.sum(summed, axis=1)
    return diag_inverse, variance
```

```python
import jax
import jax.numpy as jnp
from jax import lax
from jax.experimental import pallas as pl
from jax.experimental.pallas import tpu as pltpu
from jax.sharding import PartitionSpec as P


NZ, NH, NL, NY, NC = 4, 2, 2, 4, 2


def row_of(z, h):
    return (z % NZ) * NH + h


def col_of(l, y, j):
    return l * NY * NC + (y % NY) * NC + j


def z_shift(k):
    return [(row_of(z, h), row_of(z + k, h)) for z in range(NZ) for h in range(NH)]


H_SWAP = [(row_of(z, h), row_of(z, 1 - h)) for z in range(NZ) for h in range(NH)]
COLS = [(l, y, j) for l in range(NL) for y in range(NY) for j in range(NC)]


def y_shift(k, other_core):
    return [(col_of(l, y, j), col_of(l, y + k, j ^ other_core(l, (y + k) % NY))) for l, y, j in COLS]


L_SWAP = [(col_of(l, y, j), col_of(1 - l, y, j if l == 0 else 1 - j)) for l, y, j in COLS]
CORE_SWAP = [(col_of(l, y, j), col_of(l, y, 1 - j)) for l, y, j in COLS]


def same_core(la, ya, lb, yb):
    dy = (yb - ya) % NY
    near = jnp.where(dy == 2, yb >= 2, dy != 3)
    return jnp.where(la != lb, lb == 1, near).astype(jnp.int32)


def device(r, c):
    return r * (NL * NY * NC) + c


def spare_moves():
    cross, up, down, far = [], [], [], []
    for l, y, j in COLS:
        owner = l * NY + y
        z, h = owner // NH, owner % NH
        c = col_of(l, y, j)
        if j != h:
            cross.append((device(row_of(z, h), c), device(row_of(z, j), c)))
        up.append((device(row_of(z, j), c), device(row_of(z + 1, j), c)))
        down.append((device(row_of(z, j), c), device(row_of(z - 1, j), c)))
        far.append((device(row_of(z + 1, j), c), device(row_of(z + 2, j), c)))
    return cross, up, down, far


SPARE = spare_moves()
TN = (((0,), (0,)), ((), ()))
UPPER = [(i, j) for i in range(4) for j in range(i, 4)]


def halves(x):
    high = x.astype(jnp.bfloat16)
    return high, (x - high.astype(jnp.float32)).astype(jnp.bfloat16)


def dot3(a, b):
    ah, al = a
    bh, bl = b

    def dot(x, y):
        return lax.dot_general(x, y, TN, preferred_element_type=jnp.float32)

    return dot(ah, bh) + (dot(ah, bl) + dot(al, bh))


def couple_kernel(which, scale, *refs):
    a_in, l_in, e_in = refs[0:8], refs[8:17], refs[17:21]
    out, a_buf, l_buf, acc, a_sem, l_sem = refs[21:]
    p = acc.shape[0]
    q = p // 4
    for k in range(8):
        pltpu.make_async_copy(a_in[k], a_buf.at[k], a_sem.at[k]).start()
        for s in range(8):

            @pl.when(which[k] == s)
            def _():
                pltpu.make_async_copy(l_in[s], l_buf.at[k], l_sem.at[k]).start()

    for s in range(4):

        @pl.when(which[8] == s)
        def _():
            pltpu.make_async_copy(e_in[s], a_buf.at[8], a_sem.at[8]).start()

    pltpu.make_async_copy(l_in[8], l_buf.at[8], l_sem.at[8]).start()
    pltpu.make_async_copy(l_in[0], l_buf.at[9], l_sem.at[9]).start()
    acc[...] = jnp.zeros_like(acc)

    @pl.loop(0, 9)
    def _(k):
        pltpu.make_async_copy(a_in[0], a_buf.at[k], a_sem.at[k]).wait()
        pltpu.make_async_copy(l_in[0], l_buf.at[k], l_sem.at[k]).wait()
        acc[...] += dot3(halves(a_buf[k] * scale[k]), halves(l_buf[k]))

    pltpu.make_async_copy(l_in[0], l_buf.at[9], l_sem.at[9]).wait()
    half = dot3(halves(l_buf[9] * scale[9]), halves(acc[...]))
    acc[...] = half
    for n, (i, j) in enumerate(UPPER):
        rows, cols = slice(i * q, (i + 1) * q), slice(j * q, (j + 1) * q)
        out[pl.ds((n // 2) * q, q), pl.ds((n % 2) * q, q)] = acc[rows, cols] + acc[cols, rows].T


def couple(which, scale, a_list, l_list, e_list):
    p = a_list[0].shape[0]
    anywhere = pl.BlockSpec(memory_space=pl.ANY)
    scalars = pl.BlockSpec(memory_space=pltpu.SMEM)
    count = len(a_list) + len(l_list) + len(e_list)
    return pl.pallas_call(
        couple_kernel,
        out_shape=jax.ShapeDtypeStruct((5 * (p // 4), p // 2), jnp.float32),
        in_specs=[scalars, scalars] + [anywhere] * count,
        out_specs=pl.BlockSpec(memory_space=pltpu.VMEM),
        scratch_shapes=[
            pltpu.VMEM((9, p, p), jnp.float32),
            pltpu.VMEM((10, p, p), jnp.float32),
            pltpu.VMEM((p, p), jnp.float32),
            pltpu.SemaphoreType.DMA((9,)),
            pltpu.SemaphoreType.DMA((10,)),
        ],
        compiler_params=pltpu.CompilerParams(vmem_limit_bytes=40 << 20),
        cost_estimate=pl.CostEstimate(flops=60 * p**3, bytes_accessed=19 * p * p * 4, transcendentals=0),
        name="couple",
    )(which, scale, *a_list, *l_list, *e_list)


def unpack_kernel(packed, d, out):
    p = d.shape[0]
    q = p // 4
    for n, (i, j) in enumerate(UPPER):
        rows, cols = slice(i * q, (i + 1) * q), slice(j * q, (j + 1) * q)
        block = packed[pl.ds((n // 2) * q, q), pl.ds((n % 2) * q, q)]
        out[rows, cols] = d[rows, cols] + block
        if i != j:
            out[cols, rows] = d[cols, rows] + block.T


def unpack(packed, d):
    return pl.pallas_call(
        unpack_kernel,
        out_shape=jax.ShapeDtypeStruct(d.shape, jnp.float32),
        in_specs=[pl.BlockSpec(memory_space=pltpu.VMEM)] * 2,
        out_specs=pl.BlockSpec(memory_space=pltpu.VMEM),
        name="unpack",
    )(packed, d)


def shards(inverse_anc, factor, pattern, d_inverse, jac_blocks, jac_values):
    p = factor.shape[0]
    n_row = lax.axis_size("row")
    n_col = lax.axis_size("col")
    r = lax.axis_index("row")
    c = lax.axis_index("col")
    z, h = r // NH, r % NH
    l, y, j = c // (NY * NC), (c // NC) % NY, c % NC
    owner = c // NC

    def hop(x, axis, moves):
        return lax.ppermute(x, axis, moves)

    both = ("row", "col")
    take = jnp.where(same_core(r // NY, r % NY, l, y) == 1, j, 1 - j)
    a0 = lax.dynamic_slice_in_dim(inverse_anc, take * p, p, 0)
    spare = lax.dynamic_slice_in_dim(inverse_anc, (1 - take) * p, p, 0)

    a1 = hop(a0, "row", H_SWAP)
    a0m, a0p = hop(a0, "row", z_shift(1)), hop(a0, "row", z_shift(-1))
    a1m, a1p = hop(a1, "row", z_shift(1)), hop(a1, "row", z_shift(-1))
    a0f = hop(a0m, "row", z_shift(1))
    a1f = hop(a1p, "row", z_shift(-1))

    l0 = factor
    keep = lambda lb, yb: 0
    turn = lambda lb, yb: 1
    l1 = hop(l0, "col", L_SWAP)
    l0m, l0p = hop(l0, "col", y_shift(1, keep)), hop(l0, "col", y_shift(-1, turn))
    l1m, l1p = hop(l1, "col", y_shift(1, keep)), hop(l1, "col", y_shift(-1, keep))
    l0f = hop(l0m, "col", y_shift(1, lambda lb, yb: 0 if yb >= 2 else 1))
    l1f = hop(l1p, "col", y_shift(-1, keep))
    l_core = hop(l0, "col", CORE_SWAP)

    cross, up, down, far = SPARE
    moved = hop(spare, both, cross)
    e0 = jnp.where(j == owner % NH, spare, moved)
    e_up, e_down = hop(e0, both, up), hop(e0, both, down)
    e_far = hop(e_up, both, far)

    dz = jnp.array([0, 3, 1, 2, 0, 3, 1, 2], jnp.int32)
    dh = jnp.array([0, 0, 0, 0, 1, 1, 1, 1], jnp.int32)
    rk = ((z + dz) % NZ) * NH + (h ^ dh)
    la, ya = rk // NY, rk % NY
    slot_of_dy = jnp.array([0, 2, 3, 1], jnp.int32)
    l_slot = (la ^ l) * 4 + jnp.take(slot_of_dy, (ya - y) % NY)
    same = same_core(la, ya, l, y)
    block_k = 2 * rk + jnp.where(same == 1, j, 1 - j)
    spare_slot = jnp.take(jnp.array([0, 1, 3, 2], jnp.int32), (z - owner // NH) % NZ)
    which = jnp.concatenate([l_slot, spare_slot[None]]).astype(jnp.int32)
    own_pattern = jnp.take(pattern, r, axis=1).astype(jnp.float32)
    weight = jnp.where(rk == owner, 0.5, 1.0) * jnp.take(own_pattern, block_k)
    spare_weight = jnp.where(j == h, 1.0, 0.0) * jnp.take(own_pattern, c ^ 1)
    scale = jnp.concatenate([weight, spare_weight[None], jnp.take(own_pattern, c)[None]]).astype(jnp.float32)

    partial_value = couple(
        which,
        scale,
        [a0, a0m, a0p, a0f, a1, a1m, a1p, a1f],
        [l0, l0m, l0p, l0f, l1, l1m, l1p, l1f, l_core],
        [e0, e_up, e_down, e_far],
    )
    pieces = partial_value.reshape(n_col, -1, p // 2)
    pieces = lax.all_to_all(pieces, "col", split_axis=0, concat_axis=0, tiled=True)
    own = jnp.sum(pieces, axis=0)
    whole = lax.all_to_all(jnp.broadcast_to(own[None], pieces.shape), "col", split_axis=0, concat_axis=0, tiled=True)
    diag_block = unpack(whole.reshape(partial_value.shape), d_inverse)

    item_rows = jac_values.shape[0]
    per_item = jac_values.shape[1]
    capacity = 2 * item_rows * per_item // n_row
    flat_blocks = jac_blocks.reshape(-1)
    entries = jac_values.reshape(item_rows * per_item, p)
    onehot = (flat_blocks[:, None] == jnp.arange(n_row, dtype=jnp.int32)[None, :]).astype(jnp.int32)
    ranks = jnp.cumsum(onehot, axis=0) - 1
    position = jnp.sum(ranks * onehot, axis=1)
    slot_index = flat_blocks * capacity + position
    slotted = jnp.zeros((n_row * capacity, p), jnp.float32).at[slot_index].set(entries)
    slotted = slotted.reshape(n_row, capacity, p)
    slotted, _ = lax.optimization_barrier((slotted, a1m))
    slots_in = lax.all_to_all(slotted, "row", split_axis=0, concat_axis=0, tiled=True)
    projected = jnp.einsum("skp,pq->skq", slots_in, diag_block, precision=lax.Precision.HIGH)
    forms = jnp.sum(projected * slots_in, axis=2)
    returned = lax.all_to_all(forms, "row", split_axis=0, concat_axis=0, tiled=True)
    picked = returned.reshape(-1)[slot_index].reshape(item_rows, per_item)
    variance = jnp.sum(picked, axis=1)
    return (diag_block, variance)


def solution(mesh):
    return jax.shard_map(
        shards,
        mesh=mesh,
        in_specs=(
            P("row", "col"),
            P("col", "row"),
            P(),
            P("row", None),
            P(("row", "col"), None),
            P(("row", "col"), None, None),
        ),
        out_specs=(P("row", None), P(("row", "col"))),
        check_vma=False,
    )
```

```python
import jax
import jax.numpy as jnp
from jax import lax
from jax.experimental import pallas as pl
from jax.experimental.pallas import tpu as pltpu
from jax.sharding import PartitionSpec as P


NZ, NH, NL, NY, NC = 4, 2, 2, 4, 2


def row_of(z, h):
    return (z % NZ) * NH + h


def col_of(l, y, j):
    return l * NY * NC + (y % NY) * NC + j


def z_shift(k):
    return [(row_of(z, h), row_of(z + k, h)) for z in range(NZ) for h in range(NH)]


H_SWAP = [(row_of(z, h), row_of(z, 1 - h)) for z in range(NZ) for h in range(NH)]
COLS = [(l, y, j) for l in range(NL) for y in range(NY) for j in range(NC)]


def y_shift(k, other_core):
    return [(col_of(l, y, j), col_of(l, y + k, j ^ other_core(l, (y + k) % NY))) for l, y, j in COLS]


L_SWAP = [(col_of(l, y, j), col_of(1 - l, y, j if l == 0 else 1 - j)) for l, y, j in COLS]
CORE_SWAP = [(col_of(l, y, j), col_of(l, y, 1 - j)) for l, y, j in COLS]


def same_core(la, ya, lb, yb):
    dy = lax.rem(yb - ya + NY, NY)
    near = jnp.where(dy == 2, jnp.where(yb >= 2, 1, 0), jnp.where(dy == 3, 0, 1))
    return jnp.where(la != lb, lb, near)


def coordinates():
    r, c = lax.axis_index("row"), lax.axis_index("col")
    return r // NH, r % NH, c // (NY * NC), (c // NC) % NY, c % NC


TN = (((0,), (0,)), ((), ()))
UPPER = [(i, j) for i in range(4) for j in range(i, 4)]


def halves(x):
    high = x.astype(jnp.bfloat16)
    return high, (x - high.astype(jnp.float32)).astype(jnp.bfloat16)


def dot3(a, b):
    ah, al = a
    bh, bl = b

    def dot(x, y):
        return lax.dot_general(x, y, TN, preferred_element_type=jnp.float32)

    return dot(ah, bh) + (dot(ah, bl) + dot(al, bh))


def pick_kernel(a, out, main, other, sems):
    p = main.shape[0]
    z, h, l, y, j = coordinates()
    r = z * NH + h
    take = jnp.where(same_core(r // NY, r % NY, l, y) == 1, j, 1 - j)
    first = pl.multiple_of(take * p, p)
    second = pl.multiple_of((1 - take) * p, p)
    one = pltpu.make_async_copy(a.at[pl.ds(first, p)], main, sems.at[0])
    two = pltpu.make_async_copy(a.at[pl.ds(second, p)], other, sems.at[1])
    one.start()
    two.start()
    one.wait()
    two.wait()
    on_diagonal = r == l * NY + y
    rows = lax.broadcasted_iota(jnp.int32, (p, p), 0)
    cols = lax.broadcasted_iota(jnp.int32, (p, p), 1)

    @pl.when(on_diagonal)
    def _():
        out[0:p] = jnp.where(rows <= cols, main[...], other[...])
        crossing = jnp.sum(jnp.where(rows == cols, other[...], 0.0), axis=0, keepdims=True)
        out[p : p + 8] = jnp.broadcast_to(crossing, (8, p))

    @pl.when(jnp.logical_not(on_diagonal))
    def _():
        out[0:p] = main[...]
        out[p : p + 8] = jnp.zeros((8, p), jnp.float32)


def pick(a):
    p = a.shape[1]
    return pl.pallas_call(
        pick_kernel,
        out_shape=jax.ShapeDtypeStruct((p + 8, p), jnp.float32),
        in_specs=[pl.BlockSpec(memory_space=pl.ANY)],
        out_specs=pl.BlockSpec(memory_space=pltpu.VMEM),
        scratch_shapes=[
            pltpu.VMEM((p, p), jnp.float32),
            pltpu.VMEM((p, p), jnp.float32),
            pltpu.SemaphoreType.DMA((2,)),
        ],
        cost_estimate=pl.CostEstimate(flops=0, bytes_accessed=12 * p * p, transcendentals=0),
        name="pick",
    )(a)


DZ = (0, 3, 1, 2, 0, 3, 1, 2)
DH = (0, 0, 0, 0, 1, 1, 1, 1)


def couple_kernel(pattern, *refs):
    a_in, l_in = refs[0:8], refs[8:17]
    out, a_buf, l_buf, acc, a_sem, l_sem, weight = refs[17:]
    p = acc.shape[0]
    q = p // 4
    z, h, l, y, j = coordinates()
    panel, owner = z * NH + h, l * NY + y
    diagonal = jnp.int32(0)
    for k in range(8):
        pltpu.make_async_copy(a_in[k], a_buf.at[k], a_sem.at[k]).start()
        rk = lax.rem(z + DZ[k], NZ) * NH + (h ^ DH[k])
        la, ya = rk // NY, rk % NY
        dy = lax.rem(ya - y + NY, NY)
        slot = jnp.where(la != l, 4, 0) + jnp.where(dy == 0, 0, jnp.where(dy == 3, 1, jnp.where(dy == 1, 2, 3)))
        for s in range(8):

            @pl.when(slot == s)
            def _():
                pltpu.make_async_copy(l_in[s], l_buf.at[k], l_sem.at[k]).start()

        block = 2 * rk + jnp.where(same_core(la, ya, l, y) == 1, j, 1 - j)
        weight[k] = pattern[block, panel]
        diagonal = jnp.where(rk == owner, k, diagonal)
    weight[8] = pattern[2 * owner + 1 - j, panel]
    weight[9] = pattern[2 * owner + j, panel]
    pltpu.make_async_copy(l_in[8], l_buf.at[8], l_sem.at[8]).start()
    pltpu.make_async_copy(l_in[0], l_buf.at[9], l_sem.at[9]).start()
    acc[...] = jnp.zeros_like(acc)
    rows = lax.broadcasted_iota(jnp.int32, (p, p), 0)
    cols = lax.broadcasted_iota(jnp.int32, (p, p), 1)

    def add(k):
        a = a_buf[k, 0:p] * weight[k].astype(jnp.float32)
        acc[...] += dot3(halves(a), halves(l_buf[k]))

    @pl.loop(0, 8)
    def _(k):
        pltpu.make_async_copy(a_in[0], a_buf.at[k], a_sem.at[k]).wait()
        pltpu.make_async_copy(l_in[0], l_buf.at[k], l_sem.at[k]).wait()

        @pl.when(k == diagonal)
        def _():
            both = a_buf[k, 0:p]
            crossing = a_buf[k, p : p + 1]
            a_buf[8, 0:p] = jnp.where(rows > cols, both, jnp.where(rows == cols, 0.5 * crossing, 0.0))
            a_buf[k, 0:p] = jnp.where(rows < cols, both, jnp.where(rows == cols, 0.5 * both, 0.0))

        add(k)

    pltpu.make_async_copy(l_in[0], l_buf.at[8], l_sem.at[8]).wait()
    add(8)
    pltpu.make_async_copy(l_in[0], l_buf.at[9], l_sem.at[9]).wait()
    half = dot3(halves(l_buf[9] * weight[9].astype(jnp.float32)), halves(acc[...]))
    acc[...] = half
    for n, (i, k) in enumerate(UPPER):
        rows_of, cols_of = slice(i * q, (i + 1) * q), slice(k * q, (k + 1) * q)
        out[pl.ds((n // 2) * q, q), pl.ds((n % 2) * q, q)] = acc[rows_of, cols_of] + acc[cols_of, rows_of].T


def couple(pattern, a_list, l_list):
    p = l_list[0].shape[0]
    anywhere = pl.BlockSpec(memory_space=pl.ANY)
    return pl.pallas_call(
        couple_kernel,
        out_shape=jax.ShapeDtypeStruct((5 * (p // 4), p // 2), jnp.float32),
        in_specs=[pl.BlockSpec(memory_space=pltpu.SMEM)] + [anywhere] * (len(a_list) + len(l_list)),
        out_specs=pl.BlockSpec(memory_space=pltpu.VMEM),
        scratch_shapes=[
            pltpu.VMEM((9, p + 8, p), jnp.float32),
            pltpu.VMEM((10, p, p), jnp.float32),
            pltpu.VMEM((p, p), jnp.float32),
            pltpu.SemaphoreType.DMA((8,)),
            pltpu.SemaphoreType.DMA((10,)),
            pltpu.SMEM((10,), jnp.int32),
        ],
        compiler_params=pltpu.CompilerParams(vmem_limit_bytes=40 << 20),
        cost_estimate=pl.CostEstimate(flops=60 * p**3, bytes_accessed=19 * p * p * 4, transcendentals=0),
        name="couple",
    )(pattern, *a_list, *l_list)


def thirds(x):
    high = x.astype(jnp.bfloat16)
    rest = x - high.astype(jnp.float32)
    middle = rest.astype(jnp.bfloat16)
    return high, middle, (rest - middle.astype(jnp.float32)).astype(jnp.bfloat16)


def indicator(mask):
    return jnp.where(mask, 1.0, 0.0)


def nn(x, y):
    return jnp.dot(x, y, preferred_element_type=jnp.float32)


def slot_kernel(panels, values, slotted, places):
    items = panels.shape[1]
    slots = slotted.shape[0]
    n_panels = 8
    capacity = slots // n_panels
    before = indicator(
        lax.broadcasted_iota(jnp.int32, (items, items), 0) < lax.broadcasted_iota(jnp.int32, (items, items), 1)
    ).astype(jnp.bfloat16)
    panel_of = lax.broadcasted_iota(jnp.int32, (n_panels, items), 0)
    slot_of = lax.broadcasted_iota(jnp.int32, (slots, items), 0)
    base = jnp.zeros((n_panels, 1), jnp.float32)
    total = None
    for k in range(2):
        panel = panels[k : k + 1, :]
        member = indicator(panel_of == panel)
        rank = nn(member.astype(jnp.bfloat16), before) + base
        base = base + jnp.sum(member, axis=1, keepdims=True)
        place = jnp.sum(member * rank, axis=0, keepdims=True).astype(jnp.int32)
        places[k : k + 1, :] = place
        chosen = indicator(slot_of == panel * capacity + place).astype(jnp.bfloat16)
        for piece in thirds(values[:, k, :]):
            part = nn(chosen, piece)
            total = part if total is None else total + part
    slotted[...] = total


def slot_entries(panels, values, capacity):
    items, _, p = values.shape
    return pl.pallas_call(
        slot_kernel,
        out_shape=(
            jax.ShapeDtypeStruct((8 * capacity, p), jnp.float32),
            jax.ShapeDtypeStruct((2, items), jnp.int32),
        ),
        in_specs=[pl.BlockSpec(memory_space=pltpu.VMEM)] * 2,
        out_specs=(pl.BlockSpec(memory_space=pltpu.VMEM),) * 2,
        cost_estimate=pl.CostEstimate(flops=12 * capacity * 8 * items * p, bytes_accessed=12 * items * p * 4, transcendentals=0),
        name="slot_entries",
    )(panels, values)


def forms_kernel(packed, d, x, out, forms):
    p = d.shape[0]
    q = p // 4
    capacity = forms.shape[1]
    step = 4 * capacity
    for n, (i, j) in enumerate(UPPER):
        rows, cols = slice(i * q, (i + 1) * q), slice(j * q, (j + 1) * q)
        block = packed[pl.ds((n // 2) * q, q), pl.ds((n % 2) * q, q)]
        out[rows, cols] = d[rows, cols] + block
        if i != j:
            out[cols, rows] = d[cols, rows] + block.T
    high, low = halves(out[...])
    for first in range(2):
        here = x[first * step : (first + 1) * step, :]
        x_high, x_low = halves(here)
        terms = (nn(x_high, high) + (nn(x_high, low) + nn(x_low, high))) * here
        lanes = terms[:, 0:q] + terms[:, q : 2 * q] + (terms[:, 2 * q : 3 * q] + terms[:, 3 * q :])
        for panel in range(4):
            mine = lanes[panel * capacity : (panel + 1) * capacity, :]
            forms[pl.ds(first * 4 + panel, 1), :] = jnp.sum(mine.T, axis=0, keepdims=True)


def forms_of(packed, d, x, capacity):
    p = d.shape[0]
    return pl.pallas_call(
        forms_kernel,
        out_shape=(
            jax.ShapeDtypeStruct(d.shape, jnp.float32),
            jax.ShapeDtypeStruct((8, capacity), jnp.float32),
        ),
        in_specs=[pl.BlockSpec(memory_space=pltpu.VMEM)] * 3,
        out_specs=(pl.BlockSpec(memory_space=pltpu.VMEM),) * 2,
        cost_estimate=pl.CostEstimate(flops=48 * capacity * p * p, bytes_accessed=20 * p * p, transcendentals=0),
        name="forms",
    )(packed, d, x)


def finish_kernel(panels, places, answers, out):
    n_panels, capacity = answers.shape
    items = panels.shape[1]
    panel_of = lax.broadcasted_iota(jnp.int32, (n_panels, items), 0)
    place_of = lax.broadcasted_iota(jnp.int32, (capacity, items), 0)
    pieces = thirds(answers[...])
    total = jnp.zeros((1, items), jnp.float32)
    for k in range(2):
        chosen = indicator(place_of == places[k : k + 1, :]).astype(jnp.bfloat16)
        columns = nn(pieces[0], chosen) + nn(pieces[1], chosen) + nn(pieces[2], chosen)
        member = panel_of == panels[k : k + 1, :]
        total += jnp.sum(jnp.where(member, columns, 0.0), axis=0, keepdims=True)
    out[...] = total


def finish(panels, places, answers):
    return pl.pallas_call(
        finish_kernel,
        out_shape=jax.ShapeDtypeStruct((1, panels.shape[1]), jnp.float32),
        in_specs=[pl.BlockSpec(memory_space=pltpu.VMEM)] * 3,
        out_specs=pl.BlockSpec(memory_space=pltpu.VMEM),
        name="finish",
    )(panels, places, answers)


def exchange(x, axis):
    return lax.all_to_all(x, axis, split_axis=0, concat_axis=0, tiled=True)


def body(inverse_anc, factor, pattern, d_inverse, jac_blocks, jac_values):
    p = factor.shape[0]
    n_row = lax.axis_size("row")
    n_col = lax.axis_size("col")

    panels = jac_blocks.T
    capacity = 2 * jac_values.shape[0] * jac_values.shape[1] // n_row

    def keep(lb, yb):
        return 0

    def turn(lb, yb):
        return 1

    def turn_low(lb, yb):
        return 0 if yb >= 2 else 1

    l0 = factor
    l1 = lax.ppermute(l0, "col", L_SWAP)
    l0m = lax.ppermute(l0, "col", y_shift(1, keep))
    l0p = lax.ppermute(l0, "col", y_shift(-1, turn))
    a0 = pick(inverse_anc)
    a0m = lax.ppermute(a0, "row", z_shift(1))
    a0p = lax.ppermute(a0, "row", z_shift(-1))
    l_core = lax.ppermute(l0, "col", CORE_SWAP)
    a1 = lax.ppermute(a0, "row", H_SWAP)
    l1m = lax.ppermute(l1, "col", y_shift(1, keep))
    l1p = lax.ppermute(l1, "col", y_shift(-1, keep))
    a0f = lax.ppermute(a0m, "row", z_shift(1))
    l0f = lax.ppermute(l0m, "col", y_shift(1, turn_low))
    a1m = lax.ppermute(a1, "row", z_shift(1))
    a1p = lax.ppermute(a1, "row", z_shift(-1))
    l1f = lax.ppermute(l1p, "col", y_shift(-1, keep))
    a1f = lax.ppermute(a0f, "row", H_SWAP)
    slotted, places = slot_entries(panels, jac_values, capacity)
    slots_in = exchange(slotted.reshape(n_row, capacity, p), "row")
    partial_value = couple(
        pattern,
        [a0, a0m, a0p, a0f, a1, a1m, a1p, a1f],
        [l0, l0m, l0p, l0f, l1, l1m, l1p, l1f, l_core],
    )
    pieces = partial_value.reshape(n_col, -1, p // 2)
    pieces = exchange(pieces, "col")
    own = jnp.sum(pieces, axis=0)
    whole = exchange(jnp.broadcast_to(own[None], pieces.shape), "col")
    diag_block, forms = forms_of(whole.reshape(partial_value.shape), d_inverse, slots_in.reshape(-1, p), capacity)
    answers = exchange(forms, "row")
    variance = finish(panels, places, answers).reshape(-1)
    return (diag_block, variance)


def solution(mesh):
    return jax.shard_map(
        body,
        mesh=mesh,
        in_specs=(
            P("row", "col"),
            P("col", "row"),
            P(),
            P("row", None),
            P(("row", "col"), None),
            P(("row", "col"), None, None),
        ),
        out_specs=(P("row", None), P(("row", "col"))),
        check_vma=False,
    )
```

```python
import jax
import jax.numpy as jnp
from jax import lax
from jax.experimental import pallas as pl
from jax.experimental.pallas import tpu as pltpu
from jax.sharding import PartitionSpec as P


NZ, NH, NL, NY, NC = 4, 2, 2, 4, 2


def row_of(z, h):
    return (z % NZ) * NH + h


def col_of(l, y, j):
    return l * NY * NC + (y % NY) * NC + j


def z_shift(k):
    return [(row_of(z, h), row_of(z + k, h)) for z in range(NZ) for h in range(NH)]


H_SWAP = [(row_of(z, h), row_of(z, 1 - h)) for z in range(NZ) for h in range(NH)]
COLS = [(l, y, j) for l in range(NL) for y in range(NY) for j in range(NC)]


def y_shift(k, other_core):
    return [(col_of(l, y, j), col_of(l, y + k, j ^ other_core(l, (y + k) % NY))) for l, y, j in COLS]


L_SWAP = [(col_of(l, y, j), col_of(1 - l, y, j if l == 0 else 1 - j)) for l, y, j in COLS]
CORE_SWAP = [(col_of(l, y, j), col_of(l, y, 1 - j)) for l, y, j in COLS]


def same_core(la, ya, lb, yb):
    dy = lax.rem(yb - ya + NY, NY)
    near = jnp.where(dy == 2, jnp.where(yb >= 2, 1, 0), jnp.where(dy == 3, 0, 1))
    return jnp.where(la != lb, lb, near)


def coordinates():
    r, c = lax.axis_index("row"), lax.axis_index("col")
    return r // NH, r % NH, c // (NY * NC), (c // NC) % NY, c % NC


TN = (((0,), (0,)), ((), ()))
UPPER = [(i, j) for i in range(4) for j in range(i, 4)]


def halves(x):
    high = x.astype(jnp.bfloat16)
    return high, (x - high.astype(jnp.float32)).astype(jnp.bfloat16)


def dot3(a, b):
    ah, al = a
    bh, bl = b

    def dot(x, y):
        return lax.dot_general(x, y, TN, preferred_element_type=jnp.float32)

    return dot(ah, bh) + (dot(ah, bl) + dot(al, bh))


def pick_kernel(a, out, main, other, sems):
    p = main.shape[0]
    z, h, l, y, j = coordinates()
    r = z * NH + h
    take = jnp.where(same_core(r // NY, r % NY, l, y) == 1, j, 1 - j)
    first = pl.multiple_of(take * p, p)
    second = pl.multiple_of((1 - take) * p, p)
    one = pltpu.make_async_copy(a.at[pl.ds(first, p)], main, sems.at[0])
    two = pltpu.make_async_copy(a.at[pl.ds(second, p)], other, sems.at[1])
    one.start()
    two.start()
    one.wait()
    two.wait()
    on_diagonal = r == l * NY + y
    rows = lax.broadcasted_iota(jnp.int32, (p, p), 0)
    cols = lax.broadcasted_iota(jnp.int32, (p, p), 1)

    @pl.when(on_diagonal)
    def _():
        out[0:p] = jnp.where(rows <= cols, main[...], other[...])
        crossing = jnp.sum(jnp.where(rows == cols, other[...], 0.0), axis=0, keepdims=True)
        out[p : p + 8] = jnp.broadcast_to(crossing, (8, p))

    @pl.when(jnp.logical_not(on_diagonal))
    def _():
        out[0:p] = main[...]
        out[p : p + 8] = jnp.zeros((8, p), jnp.float32)


def pick(a):
    p = a.shape[1]
    return pl.pallas_call(
        pick_kernel,
        out_shape=jax.ShapeDtypeStruct((p + 8, p), jnp.float32),
        in_specs=[pl.BlockSpec(memory_space=pl.ANY)],
        out_specs=pl.BlockSpec(memory_space=pltpu.VMEM),
        scratch_shapes=[
            pltpu.VMEM((p, p), jnp.float32),
            pltpu.VMEM((p, p), jnp.float32),
            pltpu.SemaphoreType.DMA((2,)),
        ],
        cost_estimate=pl.CostEstimate(flops=0, bytes_accessed=12 * p * p, transcendentals=0),
        name="pick",
    )(a)


DZ = (0, 3, 1, 2, 0, 3, 1, 2)
DH = (0, 0, 0, 0, 1, 1, 1, 1)
EARLY_A = (0, 1, 2, 3, 4)
EARLY_L = (0, 1, 2, 4, 5, 6, 8)


def add_products(early, pattern, a_in, l_in, a_buf, l_buf, acc, a_sem, l_sem, weight):
    p = acc.shape[0]
    z, h, l, y, j = coordinates()
    panel, owner = z * NH + h, l * NY + y
    diagonal = jnp.int32(-1)
    for k in range(8):
        rk = lax.rem(z + DZ[k], NZ) * NH + (h ^ DH[k])
        la, ya = rk // NY, rk % NY
        dy = lax.rem(ya - y + NY, NY)
        slot = jnp.where(la != l, 4, 0) + jnp.where(dy == 0, 0, jnp.where(dy == 3, 1, jnp.where(dy == 1, 2, 3)))
        ready = jnp.where(dy == 2, 0, 1) if k in EARLY_A else jnp.int32(0)
        active = ready == 1 if early else ready == 0
        if k in a_in:

            @pl.when(active)
            def _():
                pltpu.make_async_copy(a_in[k], a_buf.at[k], a_sem.at[k]).start()

            for s in range(8):
                if s in l_in:

                    @pl.when(jnp.logical_and(active, slot == s))
                    def _():
                        pltpu.make_async_copy(l_in[s], l_buf.at[k], l_sem.at[k]).start()

        block = 2 * rk + jnp.where(same_core(la, ya, l, y) == 1, j, 1 - j)
        weight[k] = pattern[block, panel]
        weight[k + 8] = jnp.where(active, 1, 0)
        diagonal = jnp.where(jnp.logical_and(rk == owner, active), k, diagonal)

    @pl.when(diagonal >= 0)
    def _():
        pltpu.make_async_copy(l_in[8], l_buf.at[8], l_sem.at[8]).start()

    acc[...] = jnp.zeros_like(acc)
    rows = lax.broadcasted_iota(jnp.int32, (p, p), 0)
    cols = lax.broadcasted_iota(jnp.int32, (p, p), 1)

    @pl.loop(0, 9)
    def _(k):
        usual = jnp.minimum(k, 7)
        spare = jnp.logical_and(k == 8, diagonal >= 0)
        active = jnp.logical_or(jnp.logical_and(k < 8, weight[usual + 8] == 1), spare)

        @pl.when(active)
        def _():
            @pl.when(k < 8)
            def _():
                pltpu.make_async_copy(a_in[0], a_buf.at[usual], a_sem.at[usual]).wait()

            pltpu.make_async_copy(l_in[0], l_buf.at[k], l_sem.at[k]).wait()

            @pl.when(k == diagonal)
            def _():
                both = a_buf[k, 0:p]
                crossing = a_buf[k, p : p + 1]
                a_buf[8, 0:p] = jnp.where(rows > cols, both, jnp.where(rows == cols, 0.5 * crossing, 0.0))
                a_buf[k, 0:p] = jnp.where(rows < cols, both, jnp.where(rows == cols, 0.5 * both, 0.0))

            factor = jnp.where(k == 8, pattern[2 * owner + 1 - j, panel], weight[usual])
            a = a_buf[k, 0:p] * factor.astype(jnp.float32)
            acc[...] += dot3(halves(a), halves(l_buf[k]))


def early_kernel(pattern, *refs):
    count = len(EARLY_A) + len(EARLY_L)
    a_in = dict(zip(EARLY_A, refs[: len(EARLY_A)]))
    l_in = dict(zip(EARLY_L, refs[len(EARLY_A) : count]))
    acc, a_buf, l_buf, a_sem, l_sem, weight = refs[count:]
    add_products(True, pattern, a_in, l_in, a_buf, l_buf, acc, a_sem, l_sem, weight)


def late_kernel(pattern, before, *refs):
    a_in = dict(enumerate(refs[0:8]))
    l_in = dict(enumerate(refs[8:17]))
    out, a_buf, l_buf, acc, sums, a_sem, l_sem, more_sem, weight = refs[17:]
    p = acc.shape[0]
    q = p // 4
    z, h, l, y, j = coordinates()
    own = pltpu.make_async_copy(l_in[0], l_buf.at[9], more_sem.at[0])
    sofar = pltpu.make_async_copy(before, sums, more_sem.at[1])
    own.start()
    sofar.start()
    add_products(False, pattern, a_in, l_in, a_buf, l_buf, acc, a_sem, l_sem, weight)
    own.wait()
    sofar.wait()
    factor = pattern[2 * (l * NY + y) + j, z * NH + h].astype(jnp.float32)
    half = dot3(halves(l_buf[9] * factor), halves(acc[...] + sums[...]))
    acc[...] = half
    for n, (i, k) in enumerate(UPPER):
        rows_of, cols_of = slice(i * q, (i + 1) * q), slice(k * q, (k + 1) * q)
        out[pl.ds((n // 2) * q, q), pl.ds((n % 2) * q, q)] = acc[rows_of, cols_of] + acc[cols_of, rows_of].T


def buffers(p, l_count):
    return [
        pltpu.VMEM((9, p + 8, p), jnp.float32),
        pltpu.VMEM((l_count, p, p), jnp.float32),
    ]


def copies():
    return [pltpu.SemaphoreType.DMA((8,)), pltpu.SemaphoreType.DMA((9,))]


def couple_early(pattern, a_list, l_list):
    p = l_list[0].shape[0]
    anywhere = pl.BlockSpec(memory_space=pl.ANY)
    return pl.pallas_call(
        early_kernel,
        out_shape=jax.ShapeDtypeStruct((p, p), jnp.float32),
        in_specs=[pl.BlockSpec(memory_space=pltpu.SMEM)] + [anywhere] * (len(EARLY_A) + len(EARLY_L)),
        out_specs=pl.BlockSpec(memory_space=pltpu.VMEM),
        scratch_shapes=buffers(p, 9) + copies() + [pltpu.SMEM((16,), jnp.int32)],
        compiler_params=pltpu.CompilerParams(vmem_limit_bytes=40 << 20),
        cost_estimate=pl.CostEstimate(flops=30 * p**3, bytes_accessed=11 * p * p * 4, transcendentals=0),
        name="couple_early",
    )(pattern, *[a_list[k] for k in EARLY_A], *[l_list[k] for k in EARLY_L])


def couple_late(pattern, before, a_list, l_list):
    p = l_list[0].shape[0]
    anywhere = pl.BlockSpec(memory_space=pl.ANY)
    return pl.pallas_call(
        late_kernel,
        out_shape=jax.ShapeDtypeStruct((5 * (p // 4), p // 2), jnp.float32),
        in_specs=[pl.BlockSpec(memory_space=pltpu.SMEM)] + [anywhere] * (1 + len(a_list) + len(l_list)),
        out_specs=pl.BlockSpec(memory_space=pltpu.VMEM),
        scratch_shapes=buffers(p, 10)
        + [pltpu.VMEM((p, p), jnp.float32)] * 2
        + copies()
        + [pltpu.SemaphoreType.DMA((2,)), pltpu.SMEM((16,), jnp.int32)],
        compiler_params=pltpu.CompilerParams(vmem_limit_bytes=40 << 20),
        cost_estimate=pl.CostEstimate(flops=40 * p**3, bytes_accessed=13 * p * p * 4, transcendentals=0),
        name="couple_late",
    )(pattern, before, *a_list, *l_list)


def thirds(x):
    high = x.astype(jnp.bfloat16)
    rest = x - high.astype(jnp.float32)
    middle = rest.astype(jnp.bfloat16)
    return high, middle, (rest - middle.astype(jnp.float32)).astype(jnp.bfloat16)


def indicator(mask):
    return jnp.where(mask, 1.0, 0.0)


def nn(x, y):
    return jnp.dot(x, y, preferred_element_type=jnp.float32)


def slot_kernel(panels, values, *outs):
    slotted, places = outs[0:8], outs[8]
    items = panels.shape[1]
    n_panels = 8
    capacity = slotted[0].shape[0]
    slots = n_panels * capacity
    z, h = coordinates()[0:2]
    before = indicator(
        lax.broadcasted_iota(jnp.int32, (items, items), 0) < lax.broadcasted_iota(jnp.int32, (items, items), 1)
    ).astype(jnp.bfloat16)
    panel_of = lax.broadcasted_iota(jnp.int32, (n_panels, items), 0)
    slot_of = lax.broadcasted_iota(jnp.int32, (slots, items), 0)
    base = jnp.zeros((n_panels, 1), jnp.float32)
    total = None
    for k in range(2):
        panel = panels[k : k + 1, :]
        member = indicator(panel_of == panel)
        rank = nn(member.astype(jnp.bfloat16), before) + base
        base = base + jnp.sum(member, axis=1, keepdims=True)
        place = jnp.sum(member * rank, axis=0, keepdims=True).astype(jnp.int32)
        places[k : k + 1, :] = place
        away = jnp.bitwise_and(panel // NH - z + NZ, NZ - 1) * NH + jnp.bitwise_xor(jnp.bitwise_and(panel, NH - 1), h)
        chosen = indicator(slot_of == away * capacity + place).astype(jnp.bfloat16)
        for piece in thirds(values[:, k, :]):
            part = nn(chosen, piece)
            total = part if total is None else total + part
    for k in range(n_panels):
        slotted[k][...] = total[k * capacity : (k + 1) * capacity]


def slot_entries(panels, values, capacity):
    items, _, p = values.shape
    return pl.pallas_call(
        slot_kernel,
        out_shape=(jax.ShapeDtypeStruct((capacity, p), jnp.float32),) * 8
        + (jax.ShapeDtypeStruct((2, items), jnp.int32),),
        in_specs=[pl.BlockSpec(memory_space=pltpu.VMEM)] * 2,
        out_specs=(pl.BlockSpec(memory_space=pltpu.VMEM),) * 9,
        cost_estimate=pl.CostEstimate(flops=12 * capacity * 8 * items * p, bytes_accessed=12 * items * p * 4, transcendentals=0),
        name="slot_entries",
    )(panels, values)


def forms_kernel(packed, d, *refs):
    xs, (out, forms) = refs[0:8], refs[8:10]
    p = d.shape[0]
    q = p // 4
    capacity = forms.shape[1]
    z, h = coordinates()[0:2]
    for n, (i, j) in enumerate(UPPER):
        rows, cols = slice(i * q, (i + 1) * q), slice(j * q, (j + 1) * q)
        block = packed[pl.ds((n // 2) * q, q), pl.ds((n % 2) * q, q)]
        out[rows, cols] = d[rows, cols] + block
        if i != j:
            out[cols, rows] = d[cols, rows] + block.T
    high, low = halves(out[...])
    for first in range(2):
        here = jnp.concatenate([x[...] for x in xs[4 * first : 4 * first + 4]], axis=0)
        x_high, x_low = halves(here)
        terms = (nn(x_high, high) + (nn(x_high, low) + nn(x_low, high))) * here
        lanes = terms[:, 0:q] + terms[:, q : 2 * q] + (terms[:, 2 * q : 3 * q] + terms[:, 3 * q :])
        for n in range(4):
            k = 4 * first + n
            mine = lanes[n * capacity : (n + 1) * capacity, :]
            source = lax.rem(z - k // NH + NZ, NZ) * NH + (h ^ (k % NH))
            forms[pl.ds(source, 1), :] = jnp.sum(mine.T, axis=0, keepdims=True)


def forms_of(packed, d, xs, capacity):
    p = d.shape[0]
    return pl.pallas_call(
        forms_kernel,
        out_shape=(
            jax.ShapeDtypeStruct(d.shape, jnp.float32),
            jax.ShapeDtypeStruct((8, capacity), jnp.float32),
        ),
        in_specs=[pl.BlockSpec(memory_space=pltpu.VMEM)] * 10,
        out_specs=(pl.BlockSpec(memory_space=pltpu.VMEM),) * 2,
        cost_estimate=pl.CostEstimate(flops=48 * capacity * p * p, bytes_accessed=20 * p * p, transcendentals=0),
        name="forms",
    )(packed, d, *xs)


def finish_kernel(panels, places, answers, out):
    n_panels, capacity = answers.shape
    items = panels.shape[1]
    panel_of = lax.broadcasted_iota(jnp.int32, (n_panels, items), 0)
    place_of = lax.broadcasted_iota(jnp.int32, (capacity, items), 0)
    pieces = thirds(answers[...])
    total = jnp.zeros((1, items), jnp.float32)
    for k in range(2):
        chosen = indicator(place_of == places[k : k + 1, :]).astype(jnp.bfloat16)
        columns = nn(pieces[0], chosen) + nn(pieces[1], chosen) + nn(pieces[2], chosen)
        member = panel_of == panels[k : k + 1, :]
        total += jnp.sum(jnp.where(member, columns, 0.0), axis=0, keepdims=True)
    out[...] = total


def finish(panels, places, answers):
    return pl.pallas_call(
        finish_kernel,
        out_shape=jax.ShapeDtypeStruct((1, panels.shape[1]), jnp.float32),
        in_specs=[pl.BlockSpec(memory_space=pltpu.VMEM)] * 3,
        out_specs=pl.BlockSpec(memory_space=pltpu.VMEM),
        name="finish",
    )(panels, places, answers)


def exchange(x, axis):
    return lax.all_to_all(x, axis, split_axis=0, concat_axis=0, tiled=True)


def body(inverse_anc, factor, pattern, d_inverse, jac_blocks, jac_values):
    p = factor.shape[0]
    n_row = lax.axis_size("row")
    n_col = lax.axis_size("col")

    panels = jac_blocks.T
    capacity = 2 * jac_values.shape[0] * jac_values.shape[1] // n_row

    def keep(lb, yb):
        return 0

    def turn(lb, yb):
        return 1

    def turn_low(lb, yb):
        return 0 if yb >= 2 else 1

    l0 = factor
    l1 = lax.ppermute(l0, "col", L_SWAP)
    l0m = lax.ppermute(l0, "col", y_shift(1, keep))
    l0p = lax.ppermute(l0, "col", y_shift(-1, turn))
    a0 = pick(inverse_anc)
    a0m = lax.ppermute(a0, "row", z_shift(1))
    a0p = lax.ppermute(a0, "row", z_shift(-1))
    l_core = lax.ppermute(l0, "col", CORE_SWAP)
    a1 = lax.ppermute(a0, "row", H_SWAP)
    l1m = lax.ppermute(l1, "col", y_shift(1, keep))
    l1p = lax.ppermute(l1, "col", y_shift(-1, keep))
    a0f = lax.ppermute(a0m, "row", z_shift(1))
    l0f = lax.ppermute(l0m, "col", y_shift(1, turn_low))
    a1m = lax.ppermute(a1, "row", z_shift(1))
    a1p = lax.ppermute(a1, "row", z_shift(-1))
    l1f = lax.ppermute(l1p, "col", y_shift(-1, keep))
    a1f = lax.ppermute(a0f, "row", H_SWAP)
    a_list = [a0, a0m, a0p, a0f, a1, a1m, a1p, a1f]
    l_list = [l0, l0m, l0p, l0f, l1, l1m, l1p, l1f, l_core]
    before = couple_early(pattern, a_list, l_list)
    partial_value = couple_late(pattern, before, a_list, l_list)
    *slotted, places = slot_entries(panels, jac_values, capacity)
    xs = [slotted[0]]
    for k in range(1, 8):
        moves = [(row_of(z, h), row_of(z + k // NH, h ^ (k % NH))) for z in range(NZ) for h in range(NH)]
        xs.append(lax.ppermute(slotted[k], "row", moves))
    pieces = partial_value.reshape(n_col, -1, p // 2)
    pieces = exchange(pieces, "col")
    own = jnp.sum(pieces, axis=0)
    whole = exchange(jnp.broadcast_to(own[None], pieces.shape), "col")
    diag_block, forms = forms_of(whole.reshape(partial_value.shape), d_inverse, xs, capacity)
    answers = exchange(forms, "row")
    variance = finish(panels, places, answers).reshape(-1)
    return (diag_block, variance)


def solution(mesh):
    return jax.shard_map(
        body,
        mesh=mesh,
        in_specs=(
            P("row", "col"),
            P("col", "row"),
            P(),
            P("row", None),
            P(("row", "col"), None),
            P(("row", "col"), None, None),
        ),
        out_specs=(P("row", None), P(("row", "col"))),
        check_vma=False,
    )
```

```python
import jax
import jax.numpy as jnp
from jax import lax
from jax.experimental import pallas as pl
from jax.experimental.pallas import tpu as pltpu
from jax.sharding import PartitionSpec as P


NZ, NH, NL, NY, NC = 4, 2, 2, 4, 2


def row_of(z, h):
    return (z % NZ) * NH + h


def col_of(l, y, j):
    return l * NY * NC + (y % NY) * NC + j


def z_shift(k):
    return [(row_of(z, h), row_of(z + k, h)) for z in range(NZ) for h in range(NH)]


H_SWAP = [(row_of(z, h), row_of(z, 1 - h)) for z in range(NZ) for h in range(NH)]
COLS = [(l, y, j) for l in range(NL) for y in range(NY) for j in range(NC)]


def y_shift(k, other_core):
    return [(col_of(l, y, j), col_of(l, y + k, j ^ other_core(l, (y + k) % NY))) for l, y, j in COLS]


L_SWAP = [(col_of(l, y, j), col_of(1 - l, y, j if l == 0 else 1 - j)) for l, y, j in COLS]
CORE_SWAP = [(col_of(l, y, j), col_of(l, y, 1 - j)) for l, y, j in COLS]


def same_core(la, ya, lb, yb):
    dy = lax.rem(yb - ya + NY, NY)
    near = jnp.where(dy == 2, jnp.where(yb >= 2, 1, 0), jnp.where(dy == 3, 0, 1))
    return jnp.where(la != lb, lb, near)


def coordinates():
    r, c = lax.axis_index("row"), lax.axis_index("col")
    return r // NH, r % NH, c // (NY * NC), (c // NC) % NY, c % NC


TN = (((0,), (0,)), ((), ()))
UPPER = [(i, j) for i in range(4) for j in range(i, 4)]


def halves(x):
    high = x.astype(jnp.bfloat16)
    return high, (x - high.astype(jnp.float32)).astype(jnp.bfloat16)


def dot3(a, b):
    ah, al = a
    bh, bl = b

    def dot(x, y):
        return lax.dot_general(x, y, TN, preferred_element_type=jnp.float32)

    return dot(ah, bh) + (dot(ah, bl) + dot(al, bh))


def pick_kernel(a, out, main, other, sems):
    p = main.shape[0]
    z, h, l, y, j = coordinates()
    r = z * NH + h
    take = jnp.where(same_core(r // NY, r % NY, l, y) == 1, j, 1 - j)
    first = pl.multiple_of(take * p, p)
    second = pl.multiple_of((1 - take) * p, p)
    one = pltpu.make_async_copy(a.at[pl.ds(first, p)], main, sems.at[0])
    two = pltpu.make_async_copy(a.at[pl.ds(second, p)], other, sems.at[1])
    one.start()
    two.start()
    one.wait()
    two.wait()
    on_diagonal = r == l * NY + y
    rows = lax.broadcasted_iota(jnp.int32, (p, p), 0)
    cols = lax.broadcasted_iota(jnp.int32, (p, p), 1)

    @pl.when(on_diagonal)
    def _():
        out[0:p] = jnp.where(rows <= cols, main[...], other[...])
        crossing = jnp.sum(jnp.where(rows == cols, other[...], 0.0), axis=0, keepdims=True)
        out[p : p + 8] = jnp.broadcast_to(crossing, (8, p))

    @pl.when(jnp.logical_not(on_diagonal))
    def _():
        out[0:p] = main[...]
        out[p : p + 8] = jnp.zeros((8, p), jnp.float32)


def pick(a):
    p = a.shape[1]
    return pl.pallas_call(
        pick_kernel,
        out_shape=jax.ShapeDtypeStruct((p + 8, p), jnp.float32),
        in_specs=[pl.BlockSpec(memory_space=pl.ANY)],
        out_specs=pl.BlockSpec(memory_space=pltpu.VMEM),
        scratch_shapes=[
            pltpu.VMEM((p, p), jnp.float32),
            pltpu.VMEM((p, p), jnp.float32),
            pltpu.SemaphoreType.DMA((2,)),
        ],
        cost_estimate=pl.CostEstimate(flops=0, bytes_accessed=12 * p * p, transcendentals=0),
        name="pick",
    )(a)


DZ = (0, 3, 1, 2, 0, 3, 1, 2)
DH = (0, 0, 0, 0, 1, 1, 1, 1)
EARLY_A = (0, 1, 2, 3, 4)
EARLY_L = (0, 1, 2, 4, 5, 6, 8)


def add_products(early, pattern, a_in, l_in, a_buf, l_buf, acc, a_sem, l_sem, weight):
    p = acc.shape[0]
    z, h, l, y, j = coordinates()
    panel, owner = z * NH + h, l * NY + y
    diagonal = jnp.int32(-1)
    for k in range(8):
        rk = lax.rem(z + DZ[k], NZ) * NH + (h ^ DH[k])
        la, ya = rk // NY, rk % NY
        dy = lax.rem(ya - y + NY, NY)
        slot = jnp.where(la != l, 4, 0) + jnp.where(dy == 0, 0, jnp.where(dy == 3, 1, jnp.where(dy == 1, 2, 3)))
        ready = jnp.where(dy == 2, 0, 1) if k in EARLY_A else jnp.int32(0)
        active = ready == 1 if early else ready == 0
        if k in a_in:

            @pl.when(active)
            def _():
                start = 0
                for part in a_in[k]:
                    stop = start + part.shape[0]
                    pltpu.make_async_copy(part, a_buf.at[k, start:stop], a_sem.at[k]).start()
                    start = stop

            for s in range(8):
                if s in l_in:

                    @pl.when(jnp.logical_and(active, slot == s))
                    def _():
                        pltpu.make_async_copy(l_in[s], l_buf.at[k], l_sem.at[k]).start()

        block = 2 * rk + jnp.where(same_core(la, ya, l, y) == 1, j, 1 - j)
        weight[k] = pattern[block, panel]
        weight[k + 8] = jnp.where(active, 1, 0)
        diagonal = jnp.where(jnp.logical_and(rk == owner, active), k, diagonal)

    @pl.when(diagonal >= 0)
    def _():
        pltpu.make_async_copy(l_in[8], l_buf.at[8], l_sem.at[8]).start()

    acc[...] = jnp.zeros_like(acc)
    rows = lax.broadcasted_iota(jnp.int32, (p, p), 0)
    cols = lax.broadcasted_iota(jnp.int32, (p, p), 1)

    @pl.loop(0, 9)
    def _(k):
        usual = jnp.minimum(k, 7)
        spare = jnp.logical_and(k == 8, diagonal >= 0)
        active = jnp.logical_or(jnp.logical_and(k < 8, weight[usual + 8] == 1), spare)

        @pl.when(active)
        def _():
            @pl.when(k < 8)
            def _():
                pltpu.make_async_copy(a_in[0][0], a_buf.at[usual], a_sem.at[usual]).wait()

            pltpu.make_async_copy(l_in[0], l_buf.at[k], l_sem.at[k]).wait()

            @pl.when(k == diagonal)
            def _():
                both = a_buf[k, 0:p]
                crossing = a_buf[k, p : p + 1]
                a_buf[8, 0:p] = jnp.where(rows > cols, both, jnp.where(rows == cols, 0.5 * crossing, 0.0))
                a_buf[k, 0:p] = jnp.where(rows < cols, both, jnp.where(rows == cols, 0.5 * both, 0.0))

            factor = jnp.where(k == 8, pattern[2 * owner + 1 - j, panel], weight[usual])
            a = a_buf[k, 0:p] * factor.astype(jnp.float32)
            acc[...] += dot3(halves(a), halves(l_buf[k]))


def grouped(slots, refs):
    groups = {}
    for k in slots:
        count = 2 if k in (3, 7) else 1
        groups[k], refs = refs[:count], refs[count:]
    return groups, refs


def flat(a_list, slots):
    return [part for k in slots for part in a_list[k]]


def early_kernel(pattern, *refs):
    a_in, refs = grouped(EARLY_A, refs)
    l_in = dict(zip(EARLY_L, refs))
    count = len(EARLY_L)
    acc, a_buf, l_buf, a_sem, l_sem, weight = refs[count:]
    add_products(True, pattern, a_in, l_in, a_buf, l_buf, acc, a_sem, l_sem, weight)


def late_kernel(pattern, before, *refs):
    a_in, refs = grouped(range(8), refs)
    l_in = dict(enumerate(refs[0:9]))
    out, a_buf, l_buf, acc, sums, a_sem, l_sem, more_sem, weight = refs[9:]
    p = acc.shape[0]
    q = p // 4
    z, h, l, y, j = coordinates()
    own = pltpu.make_async_copy(l_in[0], l_buf.at[9], more_sem.at[0])
    sofar = pltpu.make_async_copy(before, sums, more_sem.at[1])
    own.start()
    sofar.start()
    add_products(False, pattern, a_in, l_in, a_buf, l_buf, acc, a_sem, l_sem, weight)
    own.wait()
    sofar.wait()
    factor = pattern[2 * (l * NY + y) + j, z * NH + h].astype(jnp.float32)
    half = dot3(halves(l_buf[9] * factor), halves(acc[...] + sums[...]))
    acc[...] = half
    for n, (i, k) in enumerate(UPPER):
        rows_of, cols_of = slice(i * q, (i + 1) * q), slice(k * q, (k + 1) * q)
        out[pl.ds((n // 2) * q, q), pl.ds((n % 2) * q, q)] = acc[rows_of, cols_of] + acc[cols_of, rows_of].T


def buffers(p, l_count):
    return [
        pltpu.VMEM((9, p + 8, p), jnp.float32),
        pltpu.VMEM((l_count, p, p), jnp.float32),
    ]


def copies():
    return [pltpu.SemaphoreType.DMA((8,)), pltpu.SemaphoreType.DMA((9,))]


def couple_early(pattern, a_list, l_list):
    p = l_list[0].shape[0]
    anywhere = pl.BlockSpec(memory_space=pl.ANY)
    return pl.pallas_call(
        early_kernel,
        out_shape=jax.ShapeDtypeStruct((p, p), jnp.float32),
        in_specs=[pl.BlockSpec(memory_space=pltpu.SMEM)] + [anywhere] * (len(flat(a_list, EARLY_A)) + len(EARLY_L)),
        out_specs=pl.BlockSpec(memory_space=pltpu.VMEM),
        scratch_shapes=buffers(p, 9) + copies() + [pltpu.SMEM((16,), jnp.int32)],
        compiler_params=pltpu.CompilerParams(vmem_limit_bytes=40 << 20),
        cost_estimate=pl.CostEstimate(flops=30 * p**3, bytes_accessed=11 * p * p * 4, transcendentals=0),
        name="couple_early",
    )(pattern, *flat(a_list, EARLY_A), *[l_list[k] for k in EARLY_L])


def couple_late(pattern, before, a_list, l_list):
    p = l_list[0].shape[0]
    anywhere = pl.BlockSpec(memory_space=pl.ANY)
    return pl.pallas_call(
        late_kernel,
        out_shape=jax.ShapeDtypeStruct((5 * (p // 4), p // 2), jnp.float32),
        in_specs=[pl.BlockSpec(memory_space=pltpu.SMEM)] + [anywhere] * (1 + len(flat(a_list, range(8))) + len(l_list)),
        out_specs=pl.BlockSpec(memory_space=pltpu.VMEM),
        scratch_shapes=buffers(p, 10)
        + [pltpu.VMEM((p, p), jnp.float32)] * 2
        + copies()
        + [pltpu.SemaphoreType.DMA((2,)), pltpu.SMEM((16,), jnp.int32)],
        compiler_params=pltpu.CompilerParams(vmem_limit_bytes=40 << 20),
        cost_estimate=pl.CostEstimate(flops=40 * p**3, bytes_accessed=13 * p * p * 4, transcendentals=0),
        name="couple_late",
    )(pattern, before, *flat(a_list, range(8)), *l_list)


def thirds(x):
    high = x.astype(jnp.bfloat16)
    rest = x - high.astype(jnp.float32)
    middle = rest.astype(jnp.bfloat16)
    return high, middle, (rest - middle.astype(jnp.float32)).astype(jnp.bfloat16)


def indicator(mask):
    return jnp.where(mask, 1.0, 0.0)


def nn(x, y):
    return jnp.dot(x, y, preferred_element_type=jnp.float32)


def slot_kernel(panels, values, *outs):
    slotted, across, places = outs[0:4], outs[4], outs[5]
    items = panels.shape[1]
    n_panels = 8
    capacity = slotted[0].shape[0]
    slots = n_panels * capacity
    z, h = coordinates()[0:2]
    before = indicator(
        lax.broadcasted_iota(jnp.int32, (items, items), 0) < lax.broadcasted_iota(jnp.int32, (items, items), 1)
    ).astype(jnp.bfloat16)
    panel_of = lax.broadcasted_iota(jnp.int32, (n_panels, items), 0)
    slot_of = lax.broadcasted_iota(jnp.int32, (slots, items), 0)
    base = jnp.zeros((n_panels, 1), jnp.float32)
    total = None
    for k in range(2):
        panel = panels[k : k + 1, :]
        member = indicator(panel_of == panel)
        rank = nn(member.astype(jnp.bfloat16), before) + base
        base = base + jnp.sum(member, axis=1, keepdims=True)
        place = jnp.sum(member * rank, axis=0, keepdims=True).astype(jnp.int32)
        places[k : k + 1, :] = place
        away = jnp.bitwise_and(panel // NH - z + NZ, NZ - 1) + NZ * jnp.bitwise_xor(jnp.bitwise_and(panel, NH - 1), h)
        chosen = indicator(slot_of == away * capacity + place).astype(jnp.bfloat16)
        for piece in thirds(values[:, k, :]):
            part = nn(chosen, piece)
            total = part if total is None else total + part
    for k in range(NZ):
        slotted[k][...] = total[k * capacity : (k + 1) * capacity]
    across[...] = total[NZ * capacity :]


def slot_entries(panels, values, capacity):
    items, _, p = values.shape
    return pl.pallas_call(
        slot_kernel,
        out_shape=(jax.ShapeDtypeStruct((capacity, p), jnp.float32),) * NZ
        + (jax.ShapeDtypeStruct((NZ * capacity, p), jnp.float32), jax.ShapeDtypeStruct((2, items), jnp.int32)),
        in_specs=[pl.BlockSpec(memory_space=pltpu.VMEM)] * 2,
        out_specs=(pl.BlockSpec(memory_space=pltpu.VMEM),) * 6,
        cost_estimate=pl.CostEstimate(flops=12 * capacity * 8 * items * p, bytes_accessed=12 * items * p * 4, transcendentals=0),
        name="slot_entries",
    )(panels, values)


def forms_kernel(packed, d, *refs):
    xs, (out, forms) = refs[0:8], refs[8:10]
    p = d.shape[0]
    q = p // 4
    capacity = forms.shape[1]
    z, h = coordinates()[0:2]
    for n, (i, j) in enumerate(UPPER):
        rows, cols = slice(i * q, (i + 1) * q), slice(j * q, (j + 1) * q)
        block = packed[pl.ds((n // 2) * q, q), pl.ds((n % 2) * q, q)]
        out[rows, cols] = d[rows, cols] + block
        if i != j:
            out[cols, rows] = d[cols, rows] + block.T
    high, low = halves(out[...])
    for first in range(2):
        here = jnp.concatenate([x[0:capacity] for x in xs[4 * first : 4 * first + 4]], axis=0)
        x_high, x_low = halves(here)
        terms = (nn(x_high, high) + (nn(x_high, low) + nn(x_low, high))) * here
        lanes = terms[:, 0:q] + terms[:, q : 2 * q] + (terms[:, 2 * q : 3 * q] + terms[:, 3 * q :])
        for n in range(4):
            mine = lanes[n * capacity : (n + 1) * capacity, :]
            source = lax.rem(z - n + NZ, NZ) * NH + (h ^ first)
            forms[pl.ds(source, 1), :] = jnp.sum(mine.T, axis=0, keepdims=True)


def forms_of(packed, d, xs, capacity):
    p = d.shape[0]
    return pl.pallas_call(
        forms_kernel,
        out_shape=(
            jax.ShapeDtypeStruct(d.shape, jnp.float32),
            jax.ShapeDtypeStruct((8, capacity), jnp.float32),
        ),
        in_specs=[pl.BlockSpec(memory_space=pltpu.VMEM)] * 10,
        out_specs=(pl.BlockSpec(memory_space=pltpu.VMEM),) * 2,
        cost_estimate=pl.CostEstimate(flops=48 * capacity * p * p, bytes_accessed=20 * p * p, transcendentals=0),
        name="forms",
    )(packed, d, *xs)


def finish_kernel(panels, places, answers, out):
    n_panels, capacity = answers.shape
    items = panels.shape[1]
    panel_of = lax.broadcasted_iota(jnp.int32, (n_panels, items), 0)
    place_of = lax.broadcasted_iota(jnp.int32, (capacity, items), 0)
    pieces = thirds(answers[...])
    total = jnp.zeros((1, items), jnp.float32)
    for k in range(2):
        chosen = indicator(place_of == places[k : k + 1, :]).astype(jnp.bfloat16)
        columns = nn(pieces[0], chosen) + nn(pieces[1], chosen) + nn(pieces[2], chosen)
        member = panel_of == panels[k : k + 1, :]
        total += jnp.sum(jnp.where(member, columns, 0.0), axis=0, keepdims=True)
    out[...] = total


def finish(panels, places, answers):
    return pl.pallas_call(
        finish_kernel,
        out_shape=jax.ShapeDtypeStruct((1, panels.shape[1]), jnp.float32),
        in_specs=[pl.BlockSpec(memory_space=pltpu.VMEM)] * 3,
        out_specs=pl.BlockSpec(memory_space=pltpu.VMEM),
        name="finish",
    )(panels, places, answers)


def exchange(x, axis):
    return lax.all_to_all(x, axis, split_axis=0, concat_axis=0, tiled=True)


def body(inverse_anc, factor, pattern, d_inverse, jac_blocks, jac_values):
    p = factor.shape[0]
    n_row = lax.axis_size("row")
    n_col = lax.axis_size("col")

    panels = jac_blocks.T
    capacity = 2 * jac_values.shape[0] * jac_values.shape[1] // n_row

    def keep(lb, yb):
        return 0

    def turn(lb, yb):
        return 1

    def turn_low(lb, yb):
        return 0 if yb >= 2 else 1

    l0 = factor
    l1 = lax.ppermute(l0, "col", L_SWAP)
    l0m = lax.ppermute(l0, "col", y_shift(1, keep))
    l0p = lax.ppermute(l0, "col", y_shift(-1, turn))
    a0 = pick(inverse_anc)
    a0m = lax.ppermute(a0, "row", z_shift(1))
    a0p = lax.ppermute(a0, "row", z_shift(-1))
    l_core = lax.ppermute(l0, "col", CORE_SWAP)
    a1 = lax.ppermute(a0, "row", H_SWAP)
    l1m = lax.ppermute(l1, "col", y_shift(1, keep))
    l1p = lax.ppermute(l1, "col", y_shift(-1, keep))
    cut = (p // 16 + 1) * 8
    a0f = (lax.ppermute(a0m[:cut], "row", z_shift(1)), lax.ppermute(a0p[cut:], "row", z_shift(-1)))
    l0f = lax.ppermute(l0m, "col", y_shift(1, turn_low))
    a1m = lax.ppermute(a1, "row", z_shift(1))
    a1p = lax.ppermute(a1, "row", z_shift(-1))
    l1f = lax.ppermute(l1p, "col", y_shift(-1, keep))
    a1f = (lax.ppermute(a0f[0], "row", H_SWAP), lax.ppermute(a0f[1], "row", H_SWAP))
    a_list = [(a0,), (a0m,), (a0p,), a0f, (a1,), (a1m,), (a1p,), a1f]
    l_list = [l0, l0m, l0p, l0f, l1, l1m, l1p, l1f, l_core]
    before = couple_early(pattern, a_list, l_list)
    partial_value = couple_late(pattern, before, a_list, l_list)
    *slotted, across, places = slot_entries(panels, jac_values, capacity)
    crossed = lax.ppermute(across, "row", H_SWAP)
    xs = [slotted[0]] + [lax.ppermute(slotted[k], "row", z_shift(k)) for k in range(1, NZ)] + [crossed]
    for k in range(1, NZ):
        xs.append(lax.ppermute(crossed[k * capacity : (k + 1) * capacity], "row", z_shift(k)))
    pieces = partial_value.reshape(n_col, -1, p // 2)
    pieces = exchange(pieces, "col")
    own = jnp.sum(pieces, axis=0)
    whole = exchange(jnp.broadcast_to(own[None], pieces.shape), "col")
    diag_block, forms = forms_of(whole.reshape(partial_value.shape), d_inverse, xs, capacity)
    answers = exchange(forms, "row")
    variance = finish(panels, places, answers).reshape(-1)
    return (diag_block, variance)


def solution(mesh):
    return jax.shard_map(
        body,
        mesh=mesh,
        in_specs=(
            P("row", "col"),
            P("col", "row"),
            P(),
            P("row", None),
            P(("row", "col"), None),
            P(("row", "col"), None, None),
        ),
        out_specs=(P("row", None), P(("row", "col"))),
        check_vma=False,
    )
```

```python
import jax
import jax.numpy as jnp
from jax import lax
from jax.experimental import pallas as pl
from jax.experimental.pallas import tpu as pltpu
from jax.sharding import PartitionSpec as P


NZ, NH, NL, NY, NC = 4, 2, 2, 4, 2


def row_of(z, h):
    return (z % NZ) * NH + h


def col_of(l, y, j):
    return l * NY * NC + (y % NY) * NC + j


def z_shift(k):
    return [(row_of(z, h), row_of(z + k, h)) for z in range(NZ) for h in range(NH)]


H_SWAP = [(row_of(z, h), row_of(z, 1 - h)) for z in range(NZ) for h in range(NH)]
COLS = [(l, y, j) for l in range(NL) for y in range(NY) for j in range(NC)]


def y_shift(k, other_core):
    return [(col_of(l, y, j), col_of(l, y + k, j ^ other_core(l, (y + k) % NY))) for l, y, j in COLS]


L_SWAP = [(col_of(l, y, j), col_of(1 - l, y, j if l == 0 else 1 - j)) for l, y, j in COLS]
CORE_SWAP = [(col_of(l, y, j), col_of(l, y, 1 - j)) for l, y, j in COLS]


def same_core(la, ya, lb, yb):
    dy = lax.rem(yb - ya + NY, NY)
    near = jnp.where(dy == 2, jnp.where(yb >= 2, 1, 0), jnp.where(dy == 3, 0, 1))
    return jnp.where(la != lb, lb, near)


def coordinates():
    r, c = lax.axis_index("row"), lax.axis_index("col")
    return r // NH, r % NH, c // (NY * NC), (c // NC) % NY, c % NC


TN = (((0,), (0,)), ((), ()))
UPPER = [(i, j) for i in range(4) for j in range(i, 4)]


def halves(x):
    high = x.astype(jnp.bfloat16)
    return high, (x - high.astype(jnp.float32)).astype(jnp.bfloat16)


def dot3(a, b):
    ah, al = a
    bh, bl = b

    def dot(x, y):
        return lax.dot_general(x, y, TN, preferred_element_type=jnp.float32)

    return dot(ah, bh) + (dot(ah, bl) + dot(al, bh))


def pick_kernel(a, out, main, other, sems):
    p = main.shape[0]
    z, h, l, y, j = coordinates()
    r = z * NH + h
    take = jnp.where(same_core(r // NY, r % NY, l, y) == 1, j, 1 - j)
    first = pl.multiple_of(take * p, p)
    second = pl.multiple_of((1 - take) * p, p)
    one = pltpu.make_async_copy(a.at[pl.ds(first, p)], main, sems.at[0])
    two = pltpu.make_async_copy(a.at[pl.ds(second, p)], other, sems.at[1])
    one.start()
    two.start()
    one.wait()
    two.wait()
    on_diagonal = r == l * NY + y
    rows = lax.broadcasted_iota(jnp.int32, (p, p), 0)
    cols = lax.broadcasted_iota(jnp.int32, (p, p), 1)

    @pl.when(on_diagonal)
    def _():
        out[0:p] = jnp.where(rows <= cols, main[...], other[...])
        crossing = jnp.sum(jnp.where(rows == cols, other[...], 0.0), axis=0, keepdims=True)
        out[p : p + 8] = jnp.broadcast_to(crossing, (8, p))

    @pl.when(jnp.logical_not(on_diagonal))
    def _():
        out[0:p] = main[...]
        out[p : p + 8] = jnp.zeros((8, p), jnp.float32)


def pick(a):
    p = a.shape[1]
    return pl.pallas_call(
        pick_kernel,
        out_shape=jax.ShapeDtypeStruct((p + 8, p), jnp.float32),
        in_specs=[pl.BlockSpec(memory_space=pl.ANY)],
        out_specs=pl.BlockSpec(memory_space=pltpu.VMEM),
        scratch_shapes=[
            pltpu.VMEM((p, p), jnp.float32),
            pltpu.VMEM((p, p), jnp.float32),
            pltpu.SemaphoreType.DMA((2,)),
        ],
        cost_estimate=pl.CostEstimate(flops=0, bytes_accessed=12 * p * p, transcendentals=0),
        name="pick",
    )(a)


DZ = (0, 3, 1, 2, 0, 3, 1, 2)
DH = (0, 0, 0, 0, 1, 1, 1, 1)
EARLY_A = (0, 1, 2, 3, 4)
EARLY_L = (0, 1, 2, 4, 5, 6, 8)


AHEAD = 2


def add_products(early, pattern, a_in, l_in, a_buf, l_buf, acc, a_sem, l_sem, table):
    p = acc.shape[0]
    z, h, l, y, j = coordinates()
    panel, owner = z * NH + h, l * NY + y
    stored = pattern[2 * owner + j, panel]
    diagonal = jnp.int32(-1)
    count = jnp.int32(0)
    for k in range(8):
        rk = lax.rem(z + DZ[k], NZ) * NH + (h ^ DH[k])
        la, ya = rk // NY, rk % NY
        dy = lax.rem(ya - y + NY, NY)
        slot = jnp.where(la != l, 4, 0) + jnp.where(dy == 0, 0, jnp.where(dy == 3, 1, jnp.where(dy == 1, 2, 3)))
        ready = jnp.where(dy == 2, 0, 1) if k in EARLY_A else jnp.int32(0)
        active = ready == 1 if early else ready == 0
        block = 2 * rk + jnp.where(same_core(la, ya, l, y) == 1, j, 1 - j)
        table[k] = pattern[block, panel]
        table[10 + k] = slot
        diagonal = jnp.where(jnp.logical_and(rk == owner, active), k, diagonal)
        active = jnp.logical_and(active, pattern[block, panel] * stored != 0)
        table[20 + count] = k
        count = count + jnp.where(active, 1, 0)
    table[8] = pattern[2 * owner + 1 - j, panel]
    table[20 + count] = 8
    count = count + jnp.where(jnp.logical_and(diagonal >= 0, table[8] * stored != 0), 1, 0)

    def start(t):
        k = table[20 + t]
        slot = table[10 + jnp.minimum(k, 7)]
        for kk in a_in:

            @pl.when(k == kk)
            def _():
                first = 0
                for part in a_in[kk]:
                    stop = first + part.shape[0]
                    pltpu.make_async_copy(part, a_buf.at[kk, first:stop], a_sem.at[kk]).start()
                    first = stop

        for s in l_in:
            wanted = k == 8 if s == 8 else jnp.logical_and(k < 8, slot == s)

            @pl.when(wanted)
            def _():
                pltpu.make_async_copy(l_in[s], l_buf.at[k], l_sem.at[k]).start()

    for t in range(AHEAD):

        @pl.when(t < count)
        def _():
            start(t)

    acc[...] = jnp.zeros_like(acc)
    rows = lax.broadcasted_iota(jnp.int32, (p, p), 0)
    cols = lax.broadcasted_iota(jnp.int32, (p, p), 1)

    @pl.loop(0, count)
    def _(t):
        k = table[20 + t]

        @pl.when(t + AHEAD < count)
        def _():
            start(t + AHEAD)

        @pl.when(k < 8)
        def _():
            pltpu.make_async_copy(a_in[0][0], a_buf.at[k], a_sem.at[k]).wait()

        pltpu.make_async_copy(l_in[0], l_buf.at[k], l_sem.at[k]).wait()

        @pl.when(k == diagonal)
        def _():
            both = a_buf[k, 0:p]
            crossing = a_buf[k, p : p + 1]
            a_buf[8, 0:p] = jnp.where(rows > cols, both, jnp.where(rows == cols, 0.5 * crossing, 0.0))
            a_buf[k, 0:p] = jnp.where(rows < cols, both, jnp.where(rows == cols, 0.5 * both, 0.0))

        a_high, a_low = halves((a_buf[k, 0:p] * table[k].astype(jnp.float32)).T)
        l_high, l_low = halves(l_buf[k])
        acc[...] += nn(a_high, l_high) + (nn(a_high, l_low) + nn(a_low, l_high))


def grouped(slots, refs):
    groups = {}
    for k in slots:
        count = 2 if k in (3, 7) else 1
        groups[k], refs = refs[:count], refs[count:]
    return groups, refs


def flat(a_list, slots):
    return [part for k in slots for part in a_list[k]]


def early_kernel(pattern, *refs):
    a_in, refs = grouped(EARLY_A, refs)
    l_in = dict(zip(EARLY_L, refs))
    count = len(EARLY_L)
    acc, a_buf, l_buf, a_sem, l_sem, table = refs[count:]
    add_products(True, pattern, a_in, l_in, a_buf, l_buf, acc, a_sem, l_sem, table)


def late_kernel(pattern, before, *refs):
    a_in, refs = grouped(range(8), refs)
    l_in = dict(enumerate(refs[0:9]))
    out, a_buf, l_buf, acc, sums, a_sem, l_sem, more_sem, table = refs[9:]
    p = acc.shape[0]
    q = p // 4
    z, h, l, y, j = coordinates()
    own = pltpu.make_async_copy(l_in[0], l_buf.at[9], more_sem.at[0])
    sofar = pltpu.make_async_copy(before, sums, more_sem.at[1])
    own.start()
    sofar.start()
    add_products(False, pattern, a_in, l_in, a_buf, l_buf, acc, a_sem, l_sem, table)
    own.wait()
    sofar.wait()
    factor = pattern[2 * (l * NY + y) + j, z * NH + h].astype(jnp.float32)
    half = dot3(halves(l_buf[9] * factor), halves(acc[...] + sums[...]))
    acc[...] = half
    for n, (i, k) in enumerate(UPPER):
        rows_of, cols_of = slice(i * q, (i + 1) * q), slice(k * q, (k + 1) * q)
        out[pl.ds((n // 2) * q, q), pl.ds((n % 2) * q, q)] = acc[rows_of, cols_of] + acc[cols_of, rows_of].T


def buffers(p, l_count):
    return [
        pltpu.VMEM((9, p + 8, p), jnp.float32),
        pltpu.VMEM((l_count, p, p), jnp.float32),
    ]


def copies():
    return [pltpu.SemaphoreType.DMA((9,)), pltpu.SemaphoreType.DMA((9,))]


def couple_early(pattern, a_list, l_list):
    p = l_list[0].shape[0]
    anywhere = pl.BlockSpec(memory_space=pl.ANY)
    return pl.pallas_call(
        early_kernel,
        out_shape=jax.ShapeDtypeStruct((p, p), jnp.float32),
        in_specs=[pl.BlockSpec(memory_space=pltpu.SMEM)] + [anywhere] * (len(flat(a_list, EARLY_A)) + len(EARLY_L)),
        out_specs=pl.BlockSpec(memory_space=pltpu.VMEM),
        scratch_shapes=buffers(p, 9) + copies() + [pltpu.SMEM((32,), jnp.int32)],
        compiler_params=pltpu.CompilerParams(vmem_limit_bytes=28 << 20),
        cost_estimate=pl.CostEstimate(flops=30 * p**3, bytes_accessed=11 * p * p * 4, transcendentals=0),
        name="couple_early",
    )(pattern, *flat(a_list, EARLY_A), *[l_list[k] for k in EARLY_L])


def couple_late(pattern, before, a_list, l_list):
    p = l_list[0].shape[0]
    anywhere = pl.BlockSpec(memory_space=pl.ANY)
    return pl.pallas_call(
        late_kernel,
        out_shape=jax.ShapeDtypeStruct((5 * (p // 4), p // 2), jnp.float32),
        in_specs=[pl.BlockSpec(memory_space=pltpu.SMEM)] + [anywhere] * (1 + len(flat(a_list, range(8))) + len(l_list)),
        out_specs=pl.BlockSpec(memory_space=pltpu.VMEM),
        scratch_shapes=buffers(p, 10)
        + [pltpu.VMEM((p, p), jnp.float32)] * 2
        + copies()
        + [pltpu.SemaphoreType.DMA((2,)), pltpu.SMEM((32,), jnp.int32)],
        compiler_params=pltpu.CompilerParams(vmem_limit_bytes=28 << 20),
        cost_estimate=pl.CostEstimate(flops=40 * p**3, bytes_accessed=13 * p * p * 4, transcendentals=0),
        name="couple_late",
    )(pattern, before, *flat(a_list, range(8)), *l_list)


def thirds(x):
    high = x.astype(jnp.bfloat16)
    rest = x - high.astype(jnp.float32)
    middle = rest.astype(jnp.bfloat16)
    return high, middle, (rest - middle.astype(jnp.float32)).astype(jnp.bfloat16)


def indicator(mask):
    return jnp.where(mask, 1.0, 0.0)


def nn(x, y):
    return jnp.dot(x, y, preferred_element_type=jnp.float32)


def slot_kernel(panels, values, *outs):
    slotted, across, places = outs[0:4], outs[4], outs[5]
    items = panels.shape[1]
    n_panels = 8
    capacity = slotted[0].shape[0]
    slots = n_panels * capacity
    z, h = coordinates()[0:2]
    before = indicator(
        lax.broadcasted_iota(jnp.int32, (items, items), 0) < lax.broadcasted_iota(jnp.int32, (items, items), 1)
    ).astype(jnp.bfloat16)
    panel_of = lax.broadcasted_iota(jnp.int32, (n_panels, items), 0)
    slot_of = lax.broadcasted_iota(jnp.int32, (slots, items), 0)
    base = jnp.zeros((n_panels, 1), jnp.float32)
    total = None
    for k in range(2):
        panel = panels[k : k + 1, :]
        member = indicator(panel_of == panel)
        rank = nn(member.astype(jnp.bfloat16), before) + base
        base = base + jnp.sum(member, axis=1, keepdims=True)
        place = jnp.sum(member * rank, axis=0, keepdims=True).astype(jnp.int32)
        places[k : k + 1, :] = place
        away = jnp.bitwise_and(panel // NH - z + NZ, NZ - 1) + NZ * jnp.bitwise_xor(jnp.bitwise_and(panel, NH - 1), h)
        chosen = indicator(slot_of == away * capacity + place).astype(jnp.bfloat16)
        for piece in thirds(values[:, k, :]):
            part = nn(chosen, piece)
            total = part if total is None else total + part
    for k in range(NZ):
        slotted[k][...] = total[k * capacity : (k + 1) * capacity]
    across[...] = total[NZ * capacity :]


def slot_entries(panels, values, capacity):
    items, _, p = values.shape
    return pl.pallas_call(
        slot_kernel,
        out_shape=(jax.ShapeDtypeStruct((capacity, p), jnp.float32),) * NZ
        + (jax.ShapeDtypeStruct((NZ * capacity, p), jnp.float32), jax.ShapeDtypeStruct((2, items), jnp.int32)),
        in_specs=[pl.BlockSpec(memory_space=pltpu.VMEM)] * 2,
        out_specs=(pl.BlockSpec(memory_space=pltpu.VMEM),) * 6,
        cost_estimate=pl.CostEstimate(flops=12 * capacity * 8 * items * p, bytes_accessed=12 * items * p * 4, transcendentals=0),
        name="slot_entries",
    )(panels, values)


def forms_kernel(packed, d, *refs):
    xs, out, forms = refs[0:8], refs[8], refs[9]
    parts, total, x_buf, sems = refs[10:]
    p = d.shape[0]
    q = p // 4
    capacity = forms.shape[1]
    z, h = coordinates()[0:2]
    first_in = pltpu.make_async_copy(packed, parts, sems.at[0])
    second_in = pltpu.make_async_copy(d, total, sems.at[1])
    first_in.start()
    second_in.start()
    loads = []
    for k in range(8):
        load = pltpu.make_async_copy(xs[k].at[0:capacity], x_buf.at[k], sems.at[2 + k])
        load.start()
        loads.append(load)
    first_in.wait()
    second_in.wait()
    pieces = parts[...].reshape(-1, packed.shape[2])
    for n, (i, j) in enumerate(UPPER):
        rows, cols = slice(i * q, (i + 1) * q), slice(j * q, (j + 1) * q)
        block = pieces[(n // 2) * q : (n // 2 + 1) * q, (n % 2) * q : (n % 2 + 1) * q]
        total[rows, cols] += block
        if i != j:
            total[cols, rows] += block.T
    store = pltpu.make_async_copy(total, out, sems.at[10])
    store.start()
    high, low = halves(total[...])
    for first in range(2):
        for load in loads[4 * first : 4 * first + 4]:
            load.wait()
        here = x_buf[4 * first : 4 * first + 4].reshape(4 * capacity, p)
        x_high, x_low = halves(here)
        terms = (nn(x_high, high) + (nn(x_high, low) + nn(x_low, high))) * here
        lanes = terms[:, 0:q] + terms[:, q : 2 * q] + (terms[:, 2 * q : 3 * q] + terms[:, 3 * q :])
        for n in range(4):
            mine = lanes[n * capacity : (n + 1) * capacity, :]
            source = lax.rem(z - n + NZ, NZ) * NH + (h ^ first)
            forms[pl.ds(source, 1), :] = jnp.sum(mine.T, axis=0, keepdims=True)
    store.wait()


def forms_of(packed, d, xs, capacity):
    p = d.shape[0]
    return pl.pallas_call(
        forms_kernel,
        out_shape=(
            jax.ShapeDtypeStruct(d.shape, jnp.float32),
            jax.ShapeDtypeStruct((8, capacity), jnp.float32),
        ),
        in_specs=[pl.BlockSpec(memory_space=pl.ANY)] * 10,
        out_specs=(pl.BlockSpec(memory_space=pl.ANY), pl.BlockSpec(memory_space=pltpu.VMEM)),
        scratch_shapes=[
            pltpu.VMEM(packed.shape, jnp.float32),
            pltpu.VMEM((p, p), jnp.float32),
            pltpu.VMEM((8, capacity, p), jnp.float32),
            pltpu.SemaphoreType.DMA((11,)),
        ],
        compiler_params=pltpu.CompilerParams(vmem_limit_bytes=24 << 20),
        cost_estimate=pl.CostEstimate(flops=48 * capacity * p * p, bytes_accessed=20 * p * p, transcendentals=0),
        name="forms",
    )(packed, d, *xs)


def finish_kernel(panels, places, answers, out):
    n_panels, capacity = answers.shape
    items = panels.shape[1]
    panel_of = lax.broadcasted_iota(jnp.int32, (n_panels, items), 0)
    place_of = lax.broadcasted_iota(jnp.int32, (capacity, items), 0)
    pieces = thirds(answers[...])
    total = jnp.zeros((1, items), jnp.float32)
    for k in range(2):
        chosen = indicator(place_of == places[k : k + 1, :]).astype(jnp.bfloat16)
        columns = nn(pieces[0], chosen) + nn(pieces[1], chosen) + nn(pieces[2], chosen)
        member = panel_of == panels[k : k + 1, :]
        total += jnp.sum(jnp.where(member, columns, 0.0), axis=0, keepdims=True)
    out[...] = total


def finish(panels, places, answers):
    return pl.pallas_call(
        finish_kernel,
        out_shape=jax.ShapeDtypeStruct((1, panels.shape[1]), jnp.float32),
        in_specs=[pl.BlockSpec(memory_space=pltpu.VMEM)] * 3,
        out_specs=pl.BlockSpec(memory_space=pltpu.VMEM),
        name="finish",
    )(panels, places, answers)


def exchange(x, axis):
    return lax.all_to_all(x, axis, split_axis=0, concat_axis=0, tiled=True)


def body(inverse_anc, factor, pattern, d_inverse, jac_blocks, jac_values):
    p = factor.shape[0]
    n_row = lax.axis_size("row")
    n_col = lax.axis_size("col")

    panels = jac_blocks.T
    capacity = 2 * jac_values.shape[0] * jac_values.shape[1] // n_row

    def keep(lb, yb):
        return 0

    def turn(lb, yb):
        return 1

    def turn_low(lb, yb):
        return 0 if yb >= 2 else 1

    l0 = factor
    l1 = lax.ppermute(l0, "col", L_SWAP)
    l0m = lax.ppermute(l0, "col", y_shift(1, keep))
    l0p = lax.ppermute(l0, "col", y_shift(-1, turn))
    a0 = pick(inverse_anc)
    a0m = lax.ppermute(a0, "row", z_shift(1))
    a0p = lax.ppermute(a0, "row", z_shift(-1))
    l_core = lax.ppermute(l0, "col", CORE_SWAP)
    a1 = lax.ppermute(a0, "row", H_SWAP)
    l1m = lax.ppermute(l1, "col", y_shift(1, keep))
    l1p = lax.ppermute(l1, "col", y_shift(-1, keep))
    cut = (p // 16 + 1) * 8
    a0f = (lax.ppermute(a0m[:cut], "row", z_shift(1)), lax.ppermute(a0p[cut:], "row", z_shift(-1)))
    l0f = lax.ppermute(l0m, "col", y_shift(1, turn_low))
    a1m = lax.ppermute(a1, "row", z_shift(1))
    a1p = lax.ppermute(a1, "row", z_shift(-1))
    l1f = lax.ppermute(l1p, "col", y_shift(-1, keep))
    a1f = (lax.ppermute(a0f[0], "row", H_SWAP), lax.ppermute(a0f[1], "row", H_SWAP))
    a_list = [(a0,), (a0m,), (a0p,), a0f, (a1,), (a1m,), (a1p,), a1f]
    l_list = [l0, l0m, l0p, l0f, l1, l1m, l1p, l1f, l_core]
    before = couple_early(pattern, a_list, l_list)
    partial_value = couple_late(pattern, before, a_list, l_list)
    *slotted, across, places = slot_entries(panels, jac_values, capacity)
    crossed = lax.ppermute(across, "row", H_SWAP)
    xs = [slotted[0]] + [lax.ppermute(slotted[k], "row", z_shift(k)) for k in range(1, NZ)] + [crossed]
    for k in range(1, NZ):
        xs.append(lax.ppermute(crossed[k * capacity : (k + 1) * capacity], "row", z_shift(k)))
    pieces = partial_value.reshape(n_col, -1, p // 2)
    pieces = exchange(pieces, "col")
    own = jnp.sum(pieces, axis=0)
    whole = exchange(jnp.broadcast_to(own[None], pieces.shape), "col")
    diag_block, forms = forms_of(whole, d_inverse, xs, capacity)
    answers = exchange(forms, "row")
    variance = finish(panels, places, answers).reshape(-1)
    return (diag_block, variance)


def solution(mesh):
    return jax.shard_map(
        body,
        mesh=mesh,
        in_specs=(
            P("row", "col"),
            P("col", "row"),
            P(),
            P("row", None),
            P(("row", "col"), None),
            P(("row", "col"), None, None),
        ),
        out_specs=(P("row", None), P(("row", "col"))),
        check_vma=False,
    )
```

```python
import jax
import jax.numpy as jnp
from jax import lax
from jax.experimental import pallas as pl
from jax.experimental.pallas import tpu as pltpu
from jax.sharding import PartitionSpec as P


NZ, NH, NL, NY, NC = 4, 2, 2, 4, 2


def row_of(z, h):
    return (z % NZ) * NH + h


def col_of(l, y, j):
    return l * NY * NC + (y % NY) * NC + j


def z_shift(k):
    return [(row_of(z, h), row_of(z + k, h)) for z in range(NZ) for h in range(NH)]


H_SWAP = [(row_of(z, h), row_of(z, 1 - h)) for z in range(NZ) for h in range(NH)]
COLS = [(l, y, j) for l in range(NL) for y in range(NY) for j in range(NC)]


def y_shift(k, other_core):
    return [(col_of(l, y, j), col_of(l, y + k, j ^ other_core(l, (y + k) % NY))) for l, y, j in COLS]


L_SWAP = [(col_of(l, y, j), col_of(1 - l, y, j if l == 0 else 1 - j)) for l, y, j in COLS]
CORE_SWAP = [(col_of(l, y, j), col_of(l, y, 1 - j)) for l, y, j in COLS]


def same_core(la, ya, lb, yb):
    dy = lax.rem(yb - ya + NY, NY)
    near = jnp.where(dy == 2, jnp.where(yb >= 2, 1, 0), jnp.where(dy == 3, 0, 1))
    return jnp.where(la != lb, lb, near)


def coordinates():
    r, c = lax.axis_index("row"), lax.axis_index("col")
    return r // NH, r % NH, c // (NY * NC), (c // NC) % NY, c % NC


TN = (((0,), (0,)), ((), ()))
UPPER = [(i, j) for i in range(4) for j in range(i, 4)]


def halves(x):
    high = x.astype(jnp.bfloat16)
    return high, (x - high.astype(jnp.float32)).astype(jnp.bfloat16)


def dot3(a, b):
    ah, al = a
    bh, bl = b

    def dot(x, y):
        return lax.dot_general(x, y, TN, preferred_element_type=jnp.float32)

    return dot(ah, bh) + (dot(ah, bl) + dot(al, bh))


def pick_kernel(a, out, main, other, sems):
    p = main.shape[0]
    z, h, l, y, j = coordinates()
    r = z * NH + h
    take = jnp.where(same_core(r // NY, r % NY, l, y) == 1, j, 1 - j)
    first = pl.multiple_of(take * p, p)
    second = pl.multiple_of((1 - take) * p, p)
    one = pltpu.make_async_copy(a.at[pl.ds(first, p)], main, sems.at[0])
    two = pltpu.make_async_copy(a.at[pl.ds(second, p)], other, sems.at[1])
    one.start()
    two.start()
    one.wait()
    two.wait()
    on_diagonal = r == l * NY + y
    rows = lax.broadcasted_iota(jnp.int32, (p, p), 0)
    cols = lax.broadcasted_iota(jnp.int32, (p, p), 1)

    @pl.when(on_diagonal)
    def _():
        out[0:p] = jnp.where(rows <= cols, main[...], other[...]).T
        crossing = jnp.sum(jnp.where(rows == cols, other[...], 0.0), axis=0, keepdims=True)
        out[p : p + 8] = jnp.broadcast_to(crossing, (8, p))

    @pl.when(jnp.logical_not(on_diagonal))
    def _():
        out[0:p] = main[...].T
        out[p : p + 8] = jnp.zeros((8, p), jnp.float32)


def pick(a):
    p = a.shape[1]
    return pl.pallas_call(
        pick_kernel,
        out_shape=jax.ShapeDtypeStruct((p + 8, p), jnp.float32),
        in_specs=[pl.BlockSpec(memory_space=pl.ANY)],
        out_specs=pl.BlockSpec(memory_space=pltpu.VMEM),
        scratch_shapes=[
            pltpu.VMEM((p, p), jnp.float32),
            pltpu.VMEM((p, p), jnp.float32),
            pltpu.SemaphoreType.DMA((2,)),
        ],
        cost_estimate=pl.CostEstimate(flops=0, bytes_accessed=12 * p * p, transcendentals=0),
        name="pick",
    )(a)


DZ = (0, 3, 1, 2, 0, 3, 1, 2)
DH = (0, 0, 0, 0, 1, 1, 1, 1)
EARLY_A = (0, 1, 2, 3, 4)
EARLY_L = (0, 1, 2, 4, 5, 6, 8)


AHEAD = 4


def add_products(early, pattern, a_in, l_in, a_buf, l_buf, acc, a_sem, l_sem, table):
    p = acc.shape[0]
    z, h, l, y, j = coordinates()
    panel, owner = z * NH + h, l * NY + y
    stored = pattern[2 * owner + j, panel]
    diagonal = jnp.int32(-1)
    count = jnp.int32(0)
    for k in range(8):
        rk = lax.rem(z + DZ[k], NZ) * NH + (h ^ DH[k])
        la, ya = rk // NY, rk % NY
        dy = lax.rem(ya - y + NY, NY)
        slot = jnp.where(la != l, 4, 0) + jnp.where(dy == 0, 0, jnp.where(dy == 3, 1, jnp.where(dy == 1, 2, 3)))
        ready = jnp.where(dy == 2, 0, 1) if k in EARLY_A else jnp.int32(0)
        active = ready == 1 if early else ready == 0
        block = 2 * rk + jnp.where(same_core(la, ya, l, y) == 1, j, 1 - j)
        table[k] = pattern[block, panel]
        table[10 + k] = slot
        diagonal = jnp.where(jnp.logical_and(rk == owner, active), k, diagonal)
        active = jnp.logical_and(active, pattern[block, panel] * stored != 0)
        table[20 + count] = k
        count = count + jnp.where(active, 1, 0)
    table[8] = pattern[2 * owner + 1 - j, panel]
    table[20 + count] = 8
    count = count + jnp.where(jnp.logical_and(diagonal >= 0, table[8] * stored != 0), 1, 0)

    def start(t):
        k = table[20 + t]
        slot = table[10 + jnp.minimum(k, 7)]
        for kk in a_in:

            @pl.when(k == kk)
            def _():
                first = 0
                for part in a_in[kk]:
                    stop = first + part.shape[0]
                    pltpu.make_async_copy(part, a_buf.at[kk, first:stop], a_sem.at[kk]).start()
                    first = stop

        for s in l_in:
            wanted = k == 8 if s == 8 else jnp.logical_and(k < 8, slot == s)

            @pl.when(wanted)
            def _():
                pltpu.make_async_copy(l_in[s], l_buf.at[k], l_sem.at[k]).start()

    for t in range(AHEAD):

        @pl.when(t < count)
        def _():
            start(t)

    acc[...] = jnp.zeros_like(acc)
    rows = lax.broadcasted_iota(jnp.int32, (p, p), 0)
    cols = lax.broadcasted_iota(jnp.int32, (p, p), 1)

    @pl.loop(0, count)
    def _(t):
        k = table[20 + t]

        @pl.when(t + AHEAD < count)
        def _():
            start(t + AHEAD)

        @pl.when(k < 8)
        def _():
            pltpu.make_async_copy(a_in[0][0], a_buf.at[k], a_sem.at[k]).wait()

        pltpu.make_async_copy(l_in[0], l_buf.at[k], l_sem.at[k]).wait()

        @pl.when(k == diagonal)
        def _():
            both = a_buf[k, 0:p]
            crossing = a_buf[k, p : p + 1]
            a_buf[8, 0:p] = jnp.where(rows < cols, both, jnp.where(rows == cols, 0.5 * crossing, 0.0))
            a_buf[k, 0:p] = jnp.where(rows > cols, both, jnp.where(rows == cols, 0.5 * both, 0.0))

        a_high, a_low = halves(a_buf[k, 0:p])
        l_high, l_low = halves(l_buf[k])
        acc[...] += nn(a_high, l_high) + (nn(a_high, l_low) + nn(a_low, l_high))


def grouped(slots, refs):
    groups = {}
    for k in slots:
        count = 2 if k in (3, 7) else 1
        groups[k], refs = refs[:count], refs[count:]
    return groups, refs


def flat(a_list, slots):
    return [part for k in slots for part in a_list[k]]


def early_kernel(pattern, *refs):
    a_in, refs = grouped(EARLY_A, refs)
    l_in = dict(zip(EARLY_L, refs))
    count = len(EARLY_L)
    acc, a_buf, l_buf, a_sem, l_sem, table = refs[count:]
    add_products(True, pattern, a_in, l_in, a_buf, l_buf, acc, a_sem, l_sem, table)


def late_kernel(pattern, before, *refs):
    a_in, refs = grouped(range(8), refs)
    l_in = dict(enumerate(refs[0:9]))
    out, a_buf, l_buf, acc, sums, a_sem, l_sem, more_sem, table = refs[9:]
    p = acc.shape[0]
    q = p // 4
    z, h, l, y, j = coordinates()
    own = pltpu.make_async_copy(l_in[0], l_buf.at[9], more_sem.at[0])
    sofar = pltpu.make_async_copy(before, sums, more_sem.at[1])
    own.start()
    sofar.start()
    add_products(False, pattern, a_in, l_in, a_buf, l_buf, acc, a_sem, l_sem, table)
    own.wait()
    sofar.wait()
    factor = pattern[2 * (l * NY + y) + j, z * NH + h].astype(jnp.float32)
    half = dot3(halves(l_buf[9] * factor), halves(acc[...] + sums[...]))
    acc[...] = half
    for n, (i, k) in enumerate(UPPER):
        rows_of, cols_of = slice(i * q, (i + 1) * q), slice(k * q, (k + 1) * q)
        out[pl.ds((n // 2) * q, q), pl.ds((n % 2) * q, q)] = acc[rows_of, cols_of] + acc[cols_of, rows_of].T


def buffers(p, l_count):
    return [
        pltpu.VMEM((9, p + 8, p), jnp.float32),
        pltpu.VMEM((l_count, p, p), jnp.float32),
    ]


def copies():
    return [pltpu.SemaphoreType.DMA((9,)), pltpu.SemaphoreType.DMA((9,))]


def couple_early(pattern, a_list, l_list):
    p = l_list[0].shape[0]
    anywhere = pl.BlockSpec(memory_space=pl.ANY)
    return pl.pallas_call(
        early_kernel,
        out_shape=jax.ShapeDtypeStruct((p, p), jnp.float32),
        in_specs=[pl.BlockSpec(memory_space=pltpu.SMEM)] + [anywhere] * (len(flat(a_list, EARLY_A)) + len(EARLY_L)),
        out_specs=pl.BlockSpec(memory_space=pltpu.VMEM),
        scratch_shapes=buffers(p, 9) + copies() + [pltpu.SMEM((32,), jnp.int32)],
        compiler_params=pltpu.CompilerParams(vmem_limit_bytes=28 << 20),
        cost_estimate=pl.CostEstimate(flops=30 * p**3, bytes_accessed=11 * p * p * 4, transcendentals=0),
        name="couple_early",
    )(pattern, *flat(a_list, EARLY_A), *[l_list[k] for k in EARLY_L])


def couple_late(pattern, before, a_list, l_list):
    p = l_list[0].shape[0]
    anywhere = pl.BlockSpec(memory_space=pl.ANY)
    return pl.pallas_call(
        late_kernel,
        out_shape=jax.ShapeDtypeStruct((5 * (p // 4), p // 2), jnp.float32),
        in_specs=[pl.BlockSpec(memory_space=pltpu.SMEM)] + [anywhere] * (1 + len(flat(a_list, range(8))) + len(l_list)),
        out_specs=pl.BlockSpec(memory_space=pltpu.VMEM),
        scratch_shapes=buffers(p, 10)
        + [pltpu.VMEM((p, p), jnp.float32)] * 2
        + copies()
        + [pltpu.SemaphoreType.DMA((2,)), pltpu.SMEM((32,), jnp.int32)],
        compiler_params=pltpu.CompilerParams(vmem_limit_bytes=28 << 20),
        cost_estimate=pl.CostEstimate(flops=40 * p**3, bytes_accessed=13 * p * p * 4, transcendentals=0),
        name="couple_late",
    )(pattern, before, *flat(a_list, range(8)), *l_list)


def thirds(x):
    high = x.astype(jnp.bfloat16)
    rest = x - high.astype(jnp.float32)
    middle = rest.astype(jnp.bfloat16)
    return high, middle, (rest - middle.astype(jnp.float32)).astype(jnp.bfloat16)


def indicator(mask):
    return jnp.where(mask, 1.0, 0.0)


def nn(x, y):
    return jnp.dot(x, y, preferred_element_type=jnp.float32)


def slot_kernel(panels, values, *outs):
    slotted, across, places = outs[0:4], outs[4], outs[5]
    items = panels.shape[1]
    n_panels = 8
    capacity = slotted[0].shape[0]
    slots = n_panels * capacity
    z, h = coordinates()[0:2]
    before = indicator(
        lax.broadcasted_iota(jnp.int32, (items, items), 0) < lax.broadcasted_iota(jnp.int32, (items, items), 1)
    ).astype(jnp.bfloat16)
    panel_of = lax.broadcasted_iota(jnp.int32, (n_panels, items), 0)
    slot_of = lax.broadcasted_iota(jnp.int32, (slots, items), 0)
    base = jnp.zeros((n_panels, 1), jnp.float32)
    total = None
    for k in range(2):
        panel = panels[k : k + 1, :]
        member = indicator(panel_of == panel)
        rank = nn(member.astype(jnp.bfloat16), before) + base
        base = base + jnp.sum(member, axis=1, keepdims=True)
        place = jnp.sum(member * rank, axis=0, keepdims=True).astype(jnp.int32)
        places[k : k + 1, :] = place
        away = jnp.bitwise_and(panel // NH - z + NZ, NZ - 1) + NZ * jnp.bitwise_xor(jnp.bitwise_and(panel, NH - 1), h)
        chosen = indicator(slot_of == away * capacity + place).astype(jnp.bfloat16)
        for piece in thirds(values[:, k, :]):
            part = nn(chosen, piece)
            total = part if total is None else total + part
    for k in range(NZ):
        slotted[k][...] = total[k * capacity : (k + 1) * capacity]
    across[...] = total[NZ * capacity :]


def slot_entries(panels, values, capacity):
    items, _, p = values.shape
    return pl.pallas_call(
        slot_kernel,
        out_shape=(jax.ShapeDtypeStruct((capacity, p), jnp.float32),) * NZ
        + (jax.ShapeDtypeStruct((NZ * capacity, p), jnp.float32), jax.ShapeDtypeStruct((2, items), jnp.int32)),
        in_specs=[pl.BlockSpec(memory_space=pltpu.VMEM)] * 2,
        out_specs=(pl.BlockSpec(memory_space=pltpu.VMEM),) * 6,
        cost_estimate=pl.CostEstimate(flops=12 * capacity * 8 * items * p, bytes_accessed=12 * items * p * 4, transcendentals=0),
        name="slot_entries",
    )(panels, values)


def forms_kernel(packed, d, *refs):
    xs, out, forms = refs[0:8], refs[8], refs[9]
    parts, total, x_buf, sems = refs[10:]
    p = d.shape[0]
    q = p // 4
    capacity = forms.shape[1]
    z, h = coordinates()[0:2]
    first_in = pltpu.make_async_copy(packed, parts, sems.at[0])
    second_in = pltpu.make_async_copy(d, total, sems.at[1])
    first_in.start()
    second_in.start()
    loads = []
    for k in range(8):
        load = pltpu.make_async_copy(xs[k].at[0:capacity], x_buf.at[k], sems.at[2 + k])
        load.start()
        loads.append(load)
    first_in.wait()
    second_in.wait()
    pieces = parts[...].reshape(-1, packed.shape[2])
    for n, (i, j) in enumerate(UPPER):
        rows, cols = slice(i * q, (i + 1) * q), slice(j * q, (j + 1) * q)
        block = pieces[(n // 2) * q : (n // 2 + 1) * q, (n % 2) * q : (n % 2 + 1) * q]
        total[rows, cols] += block
        if i != j:
            total[cols, rows] += block.T
    store = pltpu.make_async_copy(total, out, sems.at[10])
    store.start()
    high, low = halves(total[...])
    for first in range(2):
        for load in loads[4 * first : 4 * first + 4]:
            load.wait()
        here = x_buf[4 * first : 4 * first + 4].reshape(4 * capacity, p)
        x_high, x_low = halves(here)
        terms = (nn(x_high, high) + (nn(x_high, low) + nn(x_low, high))) * here
        lanes = terms[:, 0:q] + terms[:, q : 2 * q] + (terms[:, 2 * q : 3 * q] + terms[:, 3 * q :])
        for n in range(4):
            mine = lanes[n * capacity : (n + 1) * capacity, :]
            source = lax.rem(z - n + NZ, NZ) * NH + (h ^ first)
            forms[pl.ds(source, 1), :] = jnp.sum(mine.T, axis=0, keepdims=True)
    store.wait()


def forms_of(packed, d, xs, capacity):
    p = d.shape[0]
    return pl.pallas_call(
        forms_kernel,
        out_shape=(
            jax.ShapeDtypeStruct(d.shape, jnp.float32),
            jax.ShapeDtypeStruct((8, capacity), jnp.float32),
        ),
        in_specs=[pl.BlockSpec(memory_space=pl.ANY)] * 10,
        out_specs=(pl.BlockSpec(memory_space=pl.ANY), pl.BlockSpec(memory_space=pltpu.VMEM)),
        scratch_shapes=[
            pltpu.VMEM(packed.shape, jnp.float32),
            pltpu.VMEM((p, p), jnp.float32),
            pltpu.VMEM((8, capacity, p), jnp.float32),
            pltpu.SemaphoreType.DMA((11,)),
        ],
        compiler_params=pltpu.CompilerParams(vmem_limit_bytes=24 << 20),
        cost_estimate=pl.CostEstimate(flops=48 * capacity * p * p, bytes_accessed=20 * p * p, transcendentals=0),
        name="forms",
    )(packed, d, *xs)


def finish_kernel(panels, places, answers, out):
    n_panels, capacity = answers.shape
    items = panels.shape[1]
    panel_of = lax.broadcasted_iota(jnp.int32, (n_panels, items), 0)
    place_of = lax.broadcasted_iota(jnp.int32, (capacity, items), 0)
    pieces = thirds(answers[...])
    total = jnp.zeros((1, items), jnp.float32)
    for k in range(2):
        chosen = indicator(place_of == places[k : k + 1, :]).astype(jnp.bfloat16)
        columns = nn(pieces[0], chosen) + nn(pieces[1], chosen) + nn(pieces[2], chosen)
        member = panel_of == panels[k : k + 1, :]
        total += jnp.sum(jnp.where(member, columns, 0.0), axis=0, keepdims=True)
    out[...] = total


def finish(panels, places, answers):
    return pl.pallas_call(
        finish_kernel,
        out_shape=jax.ShapeDtypeStruct((1, panels.shape[1]), jnp.float32),
        in_specs=[pl.BlockSpec(memory_space=pltpu.VMEM)] * 3,
        out_specs=pl.BlockSpec(memory_space=pltpu.VMEM),
        name="finish",
    )(panels, places, answers)


def exchange(x, axis):
    return lax.all_to_all(x, axis, split_axis=0, concat_axis=0, tiled=True)


def body(inverse_anc, factor, pattern, d_inverse, jac_blocks, jac_values):
    p = factor.shape[0]
    n_row = lax.axis_size("row")
    n_col = lax.axis_size("col")

    panels = jac_blocks.T
    capacity = 2 * jac_values.shape[0] * jac_values.shape[1] // n_row

    def keep(lb, yb):
        return 0

    def turn(lb, yb):
        return 1

    def turn_low(lb, yb):
        return 0 if yb >= 2 else 1

    l0 = factor
    l1 = lax.ppermute(l0, "col", L_SWAP)
    l0m = lax.ppermute(l0, "col", y_shift(1, keep))
    l0p = lax.ppermute(l0, "col", y_shift(-1, turn))
    a0 = pick(inverse_anc)
    a0m = lax.ppermute(a0, "row", z_shift(1))
    a0p = lax.ppermute(a0, "row", z_shift(-1))
    l_core = lax.ppermute(l0, "col", CORE_SWAP)
    a1 = lax.ppermute(a0, "row", H_SWAP)
    l1m = lax.ppermute(l1, "col", y_shift(1, keep))
    l1p = lax.ppermute(l1, "col", y_shift(-1, keep))
    cut = (p // 16 + 1) * 8
    a0f = (lax.ppermute(a0m[:cut], "row", z_shift(1)), lax.ppermute(a0p[cut:], "row", z_shift(-1)))
    l0f = lax.ppermute(l0m, "col", y_shift(1, turn_low))
    a1m = lax.ppermute(a1, "row", z_shift(1))
    a1p = lax.ppermute(a1, "row", z_shift(-1))
    l1f = lax.ppermute(l1p, "col", y_shift(-1, keep))
    a1f = (lax.ppermute(a0f[0], "row", H_SWAP), lax.ppermute(a0f[1], "row", H_SWAP))
    a_list = [(a0,), (a0m,), (a0p,), a0f, (a1,), (a1m,), (a1p,), a1f]
    l_list = [l0, l0m, l0p, l0f, l1, l1m, l1p, l1f, l_core]
    before = couple_early(pattern, a_list, l_list)
    partial_value = couple_late(pattern, before, a_list, l_list)
    *slotted, across, places = slot_entries(panels, jac_values, capacity)
    crossed = lax.ppermute(across, "row", H_SWAP)
    xs = [slotted[0]] + [lax.ppermute(slotted[k], "row", z_shift(k)) for k in range(1, NZ)] + [crossed]
    for k in range(1, NZ):
        xs.append(lax.ppermute(crossed[k * capacity : (k + 1) * capacity], "row", z_shift(k)))
    pieces = partial_value.reshape(n_col, -1, p // 2)
    pieces = exchange(pieces, "col")
    own = jnp.sum(pieces, axis=0)
    whole = exchange(jnp.broadcast_to(own[None], pieces.shape), "col")
    diag_block, forms = forms_of(whole, d_inverse, xs, capacity)
    answers = exchange(forms, "row")
    variance = finish(panels, places, answers).reshape(-1)
    return (diag_block, variance)


def solution(mesh):
    return jax.shard_map(
        body,
        mesh=mesh,
        in_specs=(
            P("row", "col"),
            P("col", "row"),
            P(),
            P("row", None),
            P(("row", "col"), None),
            P(("row", "col"), None, None),
        ),
        out_specs=(P("row", None), P(("row", "col"))),
        check_vma=False,
    )
```
